128 devices in a mesh: row: 8 (over x, y_hi), col: 16 (over y_lo, z, core).
Axes of the slice: x: 4, y: 4 (y_hi: 2, y_lo: 2; y = y_hi * 2 + y_lo), z: 4, core: 2. Of those that a mesh axis runs over, the one named last changes fastest.
Arguments:
- train_inputs: bfloat16 [512, 8192], P(('row', 'col')), may hold values from -6 to 6
- train_grads: bfloat16 [512, 8192], P(('row', 'col')), may hold values from -6 to 6
- query_inputs: bfloat16 [256, 8192], P(('row', 'col')), may hold values from -6 to 6
- query_grads: bfloat16 [256, 8192], P(('row', 'col')), may hold values from -6 to 6
- input_basis: bfloat16 [8192, 8192], P('row', 'col'), may hold values from -0.0625 to 0.0625
- output_basis: bfloat16 [8192, 8192], P('col', 'row'), may hold values from -0.0625 to 0.0625
- eigenvalues: float32 [8192, 8192], P('row', 'col'), may hold values from 0.5 to 5
- query_starts: int32 [16], replicated, may hold values from 0 to 255, as said below
- query_ends: int32 [16], replicated, may hold values from 1 to 256, as said below
Outputs:
- scores: float32 [16, 512], replicated
The draws below stay inside these ranges and needn't reach their ends.
Inputs may be any that keep to these rules, and one draw needn't show every extreme that they name: Query q covers the query rows query_starts[q] <= r < query_ends[q]: a nonempty span of at most 128 rows that lies inside one aligned block of 128 rows (rows k * 128 to (k + 1) * 128 - 1); spans of different queries may intersect or share a block. `query_ends`: see query_starts.
All inputs are finite; a program needn't handle non-finite values.
Results may differ from the reference program's by a relative error of at most 0.005.
Values may be sent and summed in bfloat16 or wider, within the bound.
A program may use at most 64 MiB of HBM per device.

```python
import math
import jax
import jax.numpy as jnp
from jax import lax

D_IN = 8192
D_OUT = 8192
TRAIN = 512
QROWS = 256
NQ = 16
QBLOCK = 128


def query_spans(key):
    keys = jax.random.split(jax.random.fold_in(key, 7), 3)
    blocks = jax.random.randint(keys[0], (NQ,), 0, QROWS // QBLOCK)
    offsets = jax.random.randint(keys[1], (NQ,), 0, QBLOCK)
    lengths = jax.random.randint(keys[2], (NQ,), 1, QBLOCK - offsets + 1)
    which = jnp.arange(NQ, dtype=jnp.int32)
    blocks = jnp.where(which == 0, QROWS // QBLOCK - 1, blocks)
    offsets = jnp.where(which <= 1, 0, offsets)
    lengths = jnp.where(which == 0, QBLOCK, lengths)
    starts = blocks * QBLOCK + offsets
    return (starts.astype(jnp.int32), (starts + lengths).astype(jnp.int32))


def draw_query_starts(key, part):
    return query_spans(key)[0]


def draw_query_ends(key, part):
    return query_spans(key)[1]


def shard_levels(own_key, shape, shards, least, largest):
    level, own = 1.0, jax.random.fold_in(own_key, 6)
    for position, shards_of in shards:
        heights = jnp.exp(jax.random.uniform(jax.random.fold_in(own, position), (shards_of,), jnp.float32, least / len(shards), largest / len(shards)))
        level = level * jnp.repeat(heights, shape[position] // shards_of).reshape([-1 if axis == position else 1 for axis in range(len(shape))])
    return level


def bell_draw(rng, shape, scale, bound, cuts=(), held_as=jnp.bfloat16):
    drawn = scale * jax.random.normal(rng, shape, jnp.float32)
    if cuts:
        drawn = drawn * shard_levels(rng, shape, cuts, -0.22, 0.18)
    return jnp.clip(drawn, -bound, bound).astype(held_as)


def setup_inputs(seed: int = 0) -> dict:
    seeds = jax.random.split(jax.random.key(seed), 10)
    return {
        "train_inputs": bell_draw(seeds[0], (TRAIN, D_IN), 1.0, 6.0, ((0, 128),)),
        "train_grads": bell_draw(seeds[1], (TRAIN, D_OUT), 1.0, 6.0, ((0, 128),)),
        "query_inputs": bell_draw(seeds[2], (QROWS, D_IN), 1.0, 6.0, ((0, 128),)),
        "query_grads": bell_draw(seeds[3], (QROWS, D_OUT), 1.0, 6.0, ((0, 128),)),
        "input_basis": bell_draw(seeds[4], (D_IN, D_IN), D_IN ** -0.5, 0.0625, ((0, 8), (1, 16))),
        "output_basis": bell_draw(seeds[5], (D_OUT, D_OUT), D_OUT ** -0.5, 0.0625, ((0, 16), (1, 8))),
        "eigenvalues": jnp.clip(jnp.exp(math.log(5.0) - 2.3025851 * jax.random.uniform(seeds[6], (D_OUT, D_IN), jnp.float32) ** shard_levels(seeds[6], (D_OUT, D_IN), ((0, 8), (1, 16)), -0.2, 0.2)), 0.5, 5.0),
        "query_starts": draw_query_starts(jax.random.fold_in(seeds[9], 71), 0),
        "query_ends": draw_query_ends(jax.random.fold_in(seeds[9], 71), 0),
    }


damping = 0.1

def rotate(rows, basis):
    return jnp.dot(rows, basis, preferred_element_type=jnp.float32).astype(jnp.bfloat16)

def reference(train_inputs, train_grads, query_inputs, query_grads, input_basis, output_basis, eigenvalues, query_starts, query_ends):
    train_in_rot = rotate(train_inputs, input_basis)
    query_in_rot = rotate(query_inputs, input_basis)
    train_grad_rot = rotate(train_grads, output_basis)
    query_grad_rot = rotate(query_grads, output_basis)
    grads_wide = train_grad_rot.astype(jnp.float32)
    denominator = eigenvalues + damping

    def per_query(span):
        span_start, span_end = span
        block_top = span_start // QBLOCK * QBLOCK
        grad_rows = lax.dynamic_slice_in_dim(query_grad_rot, block_top, QBLOCK, 0)
        input_rows = lax.dynamic_slice_in_dim(query_in_rot, block_top, QBLOCK, 0)
        positions = block_top + jnp.arange(QBLOCK, dtype=jnp.int32)
        inside = (positions >= span_start) & (positions < span_end)
        grad_rows = jnp.where(inside[:, None], grad_rows, jnp.zeros((), grad_rows.dtype))
        outer_sum = lax.dot_general(grad_rows, input_rows, (((0,), (0,)), ((), ())), preferred_element_type=jnp.float32)
        scaled = (outer_sum / denominator).astype(jnp.bfloat16)
        paired = lax.dot_general(train_in_rot, scaled, (((1,), (1,)), ((), ())), preferred_element_type=jnp.float32)
        return lax.optimization_barrier(jnp.sum(grads_wide * paired, axis=1))
    totals = lax.map(per_query, (query_starts, query_ends))
    return totals * (1.0 / math.sqrt(D_IN * D_OUT * QBLOCK))
```

```python
import functools
import math

import jax
import jax.numpy as jnp
from jax import lax
from jax.experimental import pallas as pl
from jax.experimental.pallas import tpu as pltpu
from jax.sharding import Mesh
from jax.sharding import PartitionSpec as P

D_IN = 8192
D_OUT = 8192
QBLOCK = 128
NQ = 16
MESH = pl.DeviceIdType.MESH
ROW = ("x", "u")
COL = ("v", "z", "k")
ALL = ("x", "u", "v", "z", "k")
damping = 0.1
BF = jnp.bfloat16
F32 = jnp.float32


def send(src, dst, send_sem, recv_sem, device):
    copy = pltpu.make_async_remote_copy(
        src_ref=src,
        dst_ref=dst,
        send_sem=send_sem,
        recv_sem=recv_sem,
        device_id=device,
        device_id_type=MESH,
    )
    copy.start()
    return copy


def one_hot(rows, cols, source):
    row = lax.broadcasted_iota(jnp.int32, (rows, cols), 0)
    col = lax.broadcasted_iota(jnp.int32, (rows, cols), 1)
    return jnp.where(col == source(row), 1.0, 0.0).astype(BF)


def compact_source(row):
    train = row // 4 * 8 + row % 4
    query = (row - 32) // 2 * 8 + 4 + (row - 32) % 2
    return jnp.where(row < 32, train, query)


def ordered_source(row, outer_is_r):
    train = row < 256
    rest = jnp.where(train, row, row - 256)
    width = jnp.where(train, 4, 2)
    pair = jnp.where(train, rest // 4, rest // 2)
    j = jnp.where(train, rest % 4, rest % 2)
    r, p = pair // 8, pair % 8
    chunk, inner = (r, p) if outer_is_r else (p, r)
    return chunk * 48 + jnp.where(train, 0, 32) + inner * width + j


def rotate_kernel(
    xi, gi, bi, bo, fi, fg,
    ra, rb, ai, ag, bsib, pi, pg, si, sg, ri, rg, ui, ug, hi, hg,
    ssem, rsem,
):
    x, u, v, z, k = (lax.axis_index(a) for a in ALL)
    r, p = x * 2 + u, v * 4 + z
    other = 1 - k

    def row_peer(d):
        q = lax.rem(r + d, 8)
        return q, {"x": q // 2, "u": lax.rem(q, 2)}

    def col_peer(d):
        q = lax.rem(p + d, 8)
        return q, {"v": q // 4, "z": lax.rem(q, 4)}

    barrier = pltpu.get_barrier_semaphore()
    for d in range(1, 8):
        for peer in (row_peer(d)[1], col_peer(d)[1]):
            pl.semaphore_signal(barrier, inc=1, device_id=peer, device_id_type=MESH)
    pl.semaphore_signal(barrier, inc=1, device_id={"k": other}, device_id_type=MESH)
    pl.semaphore_wait(barrier, 15)

    basis_copy = send(
        bo.at[:, pl.ds(pl.multiple_of(other * 512, 512), 512)], bsib,
        ssem.at[0, 0], rsem.at[0, 0], {"k": other},
    )
    first = []
    for d in range(1, 8):
        q, peer = row_peer(d)
        first.append(send(
            xi.at[:, pl.ds(pl.multiple_of(q * 1024, 1024), 1024)], ra.at[r],
            ssem.at[1, d], rsem.at[1, d], peer,
        ))
        q, peer = col_peer(d)
        first.append(send(
            gi.at[:, pl.ds(pl.multiple_of(q * 1024, 1024), 1024)], rb.at[p],
            ssem.at[2, d], rsem.at[2, d], peer,
        ))
    ra[r] = xi[:, pl.ds(pl.multiple_of(r * 1024, 1024), 1024)]
    rb[p] = gi[:, pl.ds(pl.multiple_of(p * 1024, 1024), 1024)]
    pick = one_hot(48, 64, compact_source)
    for copy in first:
        copy.wait()

    ai[k, p] = jnp.dot(pick, ra[...].reshape(64, 1024), preferred_element_type=F32).astype(BF)
    ag[k, r] = jnp.dot(pick, rb[...].reshape(64, 1024), preferred_element_type=F32).astype(BF)
    second = []
    for d in range(1, 8):
        second.append(send(
            ai.at[k, p], ai.at[k, p], ssem.at[3, d], rsem.at[3, d], col_peer(d)[1]
        ))
        second.append(send(
            ag.at[k, r], ag.at[k, r], ssem.at[4, d], rsem.at[4, d], row_peer(d)[1]
        ))
    for copy in second:
        copy.wait()
    swap = [
        send(ai.at[k], ai.at[k], ssem.at[5, 0], rsem.at[5, 0], {"k": other}),
        send(ag.at[k], ag.at[k], ssem.at[5, 1], rsem.at[5, 1], {"k": other}),
    ]
    basis_copy.wait()
    for copy in swap:
        copy.wait()

    own = pl.ds(pl.multiple_of(k * 512, 512), 512)
    far = pl.ds(pl.multiple_of(other * 512, 512), 512)
    for half in range(2):
        rows = pl.ds(half * 384, 384)
        part = jnp.dot(ai[half].reshape(384, 1024), bi[...], preferred_element_type=F32)
        for b in range(4):
            pi[b, rows] = part[:, b * 128 : (b + 1) * 128]
            si[b, rows] = part[:, b * 128 : (b + 1) * 128].astype(BF)
        block = ag.at[half]
        part = jnp.dot(
            block[:, :, own].reshape(384, 512), bo[:, own], preferred_element_type=F32
        ) + jnp.dot(block[:, :, far].reshape(384, 512), bsib[...], preferred_element_type=F32)
        for b in range(4):
            pg[b, rows] = part[:, b * 128 : (b + 1) * 128]
            sg[b, rows] = part[:, b * 128 : (b + 1) * 128].astype(BF)

    third = []
    for d in range(1, 4):
        q = lax.rem(x + d, 4)
        third.append(send(si.at[q], ri.at[d - 1], ssem.at[6, d], rsem.at[6, d], {"x": q}))
        q = lax.rem(z + d, 4)
        third.append(send(sg.at[q], rg.at[d - 1], ssem.at[7, d], rsem.at[7, d], {"z": q}))
    for copy in third:
        copy.wait()

    def total(part, got, place):
        value = part[place]
        for d in range(3):
            value = value + got[d].astype(F32)
        return value

    pi[x] = total(pi, ri, x)
    pg[z] = total(pg, rg, z)

    def half_of(part, place, which):
        return part.at[place, pl.ds(pl.multiple_of(which * 384, 384), 384)]

    fourth = [
        send(half_of(pi, x, 1 - u), ui, ssem.at[8, 0], rsem.at[8, 0], {"u": 1 - u}),
        send(half_of(pg, z, 1 - v), ug, ssem.at[8, 1], rsem.at[8, 1], {"v": 1 - v}),
    ]
    order_in = one_hot(384, 384, functools.partial(ordered_source, outer_is_r=False))
    order_out = one_hot(384, 384, functools.partial(ordered_source, outer_is_r=True))
    for copy in fourth:
        copy.wait()
    done_in = (half_of(pi, x, u)[...] + ui[...]).astype(BF)
    done_out = (half_of(pg, z, v)[...] + ug[...]).astype(BF)
    hi[x, u] = jnp.dot(order_in, done_in, preferred_element_type=F32).astype(BF)
    hg[k, z, v] = jnp.dot(order_out, done_out, preferred_element_type=F32).astype(BF)

    fifth = [
        send(hi.at[x, u], hi.at[x, u], ssem.at[9, 0], rsem.at[9, 0], {"u": 1 - u}),
        send(hg.at[k, z, v], hg.at[k, z, v], ssem.at[9, 1], rsem.at[9, 1], {"v": 1 - v}),
    ]
    for copy in fifth:
        copy.wait()
    sixth = []
    for d in range(1, 4):
        sixth.append(send(
            hi.at[x], hi.at[x], ssem.at[10, d], rsem.at[10, d], {"x": lax.rem(x + d, 4)}
        ))
        sixth.append(send(
            hg.at[k, z], hg.at[k, z], ssem.at[11, d], rsem.at[11, d], {"z": lax.rem(z + d, 4)}
        ))
    for copy in sixth:
        copy.wait()
    last = send(hg.at[k], hg.at[k], ssem.at[12, 0], rsem.at[12, 0], {"k": other})
    fi[...] = hi[...]
    last.wait()
    fg[...] = hg[...]


def rotate(xi, gi, bi, bo):
    vmem = pl.BlockSpec(memory_space=pltpu.VMEM)
    return pl.pallas_call(
        rotate_kernel,
        out_shape=(
            jax.ShapeDtypeStruct((4, 2, 384, 128), BF),
            jax.ShapeDtypeStruct((2, 4, 2, 384, 128), BF),
        ),
        in_specs=[vmem] * 4,
        out_specs=(vmem, vmem),
        scratch_shapes=[
            pltpu.VMEM((8, 8, 1024), BF),
            pltpu.VMEM((8, 8, 1024), BF),
            pltpu.VMEM((2, 8, 48, 1024), BF),
            pltpu.VMEM((2, 8, 48, 1024), BF),
            pltpu.VMEM((512, 512), BF),
            pltpu.VMEM((4, 768, 128), F32),
            pltpu.VMEM((4, 768, 128), F32),
            pltpu.VMEM((4, 768, 128), BF),
            pltpu.VMEM((4, 768, 128), BF),
            pltpu.VMEM((3, 768, 128), BF),
            pltpu.VMEM((3, 768, 128), BF),
            pltpu.VMEM((384, 128), F32),
            pltpu.VMEM((384, 128), F32),
            pltpu.VMEM((4, 2, 384, 128), BF),
            pltpu.VMEM((2, 4, 2, 384, 128), BF),
            pltpu.SemaphoreType.DMA((13, 8)),
            pltpu.SemaphoreType.DMA((13, 8)),
        ],
        compiler_params=pltpu.CompilerParams(
            collective_id=0, has_side_effects=True, vmem_limit_bytes=56 * 2**20
        ),
    )(xi, gi, bi, bo)


def score_kernel(starts, ends, fi, fg, eig, out, inverse, a_query, g_query, a_train, g_train, scaled, acc, stage, ssem, rsem):
    x, u, v, z, k = (lax.axis_index(a) for a in ALL)
    y = u * 2 + v

    def y_peer(d):
        q = lax.rem(y + d, 4)
        return {"u": q // 2, "v": lax.rem(q, 2)}

    def x_peer(d):
        return {"x": lax.rem(x + d, 4)}

    def z_peer(d):
        return {"z": lax.rem(z + d, 4)}

    barrier = pltpu.get_barrier_semaphore()
    for d in range(1, 4):
        for peer in (x_peer(d), y_peer(d), z_peer(d)):
            pl.semaphore_signal(barrier, inc=1, device_id=peer, device_id_type=MESH)
    pl.semaphore_signal(barrier, inc=1, device_id={"k": 1 - k}, device_id_type=MESH)

    inverse[...] = 1.0 / (eig[...] + damping)
    for h in range(2):
        for b in range(4):
            lanes = pl.ds(b * 128, 128)
            a_train[pl.ds(h * 256, 256), lanes] = fi[b, h, 0:256].astype(F32)
            a_query[pl.ds(h * 128, 128), lanes] = fi[b, h, 256:384].astype(F32)
            for s in range(2):
                at = s * 512 + b * 128
                g_train[pl.ds(h * 256, 256), pl.ds(at, 128)] = fg[s, b, h, 0:256]
                turned = jnp.transpose(fg[s, b, h, 256:384].astype(F32), (1, 0))
                g_query[pl.ds(at, 128), pl.ds(h * 128, 128)] = turned.astype(BF)
    acc[...] = jnp.zeros_like(acc)

    def query(q, carry):
        row = lax.broadcasted_iota(jnp.int32, (256, 512), 0)
        h, m = row // 128, row % 128
        true_row = 2 * (16 * (m // 16) + 2 * (m % 16 // 2) + h) + m % 2
        inside = (true_row >= starts[q]) & (true_row < ends[q])
        rows = jnp.where(inside, a_query[...], 0.0).astype(BF)
        for o in range(4):
            at = pl.ds(o * 256, 256)
            outer = jnp.dot(g_query[at, :], rows, preferred_element_type=F32)
            scaled[at, :] = (outer * inverse[at, :]).astype(BF)
        for t in range(2):
            at = pl.ds(t * 256, 256)
            paired = jnp.dot(g_train[at, :], scaled[...], preferred_element_type=F32)
            product = paired * a_train[at, :]
            column = jnp.sum(product, axis=1, keepdims=True)
            lane = lax.broadcasted_iota(jnp.int32, (256, 128), 1)
            acc[at, :] = jnp.where(lane == q, column, acc[at, :])
        return carry

    lax.fori_loop(0, NQ, query, 0)
    value = jnp.transpose(acc[...], (1, 0))[0:NQ]
    pl.semaphore_wait(barrier, 10)

    stage[0, k] = value
    copy = send(stage.at[0, k], stage.at[0, k], ssem.at[0, 0], rsem.at[0, 0], {"k": 1 - k})
    copy.wait()
    value = stage[0, 0] + stage[0, 1]
    for i, (place, peer) in enumerate(((z, z_peer), (x, x_peer), (y, y_peer))):
        n = i + 1
        stage[n, place] = value
        copies = [
            send(stage.at[n, place], stage.at[n, place], ssem.at[n, d], rsem.at[n, d], peer(d))
            for d in range(1, 4)
        ]
        for copy in copies:
            copy.wait()
        value = (stage[n, 0] + stage[n, 1]) + (stage[n, 2] + stage[n, 3])
    out[...] = value


def score(starts, ends, fi, fg, eig):
    vmem = pl.BlockSpec(memory_space=pltpu.VMEM)
    smem = pl.BlockSpec(memory_space=pltpu.SMEM)
    return pl.pallas_call(
        score_kernel,
        out_shape=jax.ShapeDtypeStruct((NQ, 512), F32),
        in_specs=[smem, smem, vmem, vmem, vmem],
        out_specs=vmem,
        scratch_shapes=[
            pltpu.VMEM((1024, 512), F32),
            pltpu.VMEM((256, 512), F32),
            pltpu.VMEM((1024, 256), BF),
            pltpu.VMEM((512, 512), F32),
            pltpu.VMEM((512, 1024), BF),
            pltpu.VMEM((1024, 512), BF),
            pltpu.VMEM((512, 128), F32),
            pltpu.VMEM((4, 4, NQ, 512), F32),
            pltpu.SemaphoreType.DMA((4, 4)),
            pltpu.SemaphoreType.DMA((4, 4)),
        ],
        compiler_params=pltpu.CompilerParams(
            collective_id=1, has_side_effects=True, vmem_limit_bytes=56 * 2**20
        ),
    )(starts, ends, fi, fg, eig)


def shards(
    train_inputs,
    train_grads,
    query_inputs,
    query_grads,
    input_basis,
    output_basis,
    eigenvalues,
    query_starts,
    query_ends,
):
    xi = jnp.pad(jnp.concatenate([train_inputs, query_inputs], 0), ((0, 2), (0, 0)))
    gi = jnp.pad(jnp.concatenate([train_grads, query_grads], 0), ((0, 2), (0, 0)))
    fi, fg = rotate(xi, gi, input_basis, output_basis)
    totals = score(query_starts, query_ends, fi, fg, eigenvalues)
    totals = totals.reshape(NQ, 2, 64, 4).transpose(0, 2, 1, 3).reshape(NQ, 512)
    return totals * (1.0 / math.sqrt(D_IN * D_OUT * QBLOCK))


def solution(mesh):
    split = Mesh(mesh.devices.reshape(4, 2, 2, 4, 2), ALL)
    placed = (
        P(ROW + COL, None),
        P(ROW + COL, None),
        P(ROW + COL, None),
        P(ROW + COL, None),
        P(ROW, COL),
        P(COL, ROW),
        P(ROW, COL),
        P(),
        P(),
    )
    return jax.shard_map(shards, mesh=split, in_specs=placed, out_specs=P(), check_vma=False)
```

```python
import math

import jax
import jax.numpy as jnp
from jax import lax
from jax.experimental import pallas as pl
from jax.experimental.pallas import tpu as pltpu
from jax.sharding import Mesh
from jax.sharding import PartitionSpec as P

D_IN = 8192
D_OUT = 8192
QBLOCK = 128
NQ = 16
MESH = pl.DeviceIdType.MESH
ROW = ("x", "u")
COL = ("v", "z", "k")
ALL = ("x", "u", "v", "z", "k")
damping = 0.1
BF = jnp.bfloat16
F32 = jnp.float32


def send(src, dst, send_sem, recv_sem, device):
    copy = pltpu.make_async_remote_copy(
        src_ref=src,
        dst_ref=dst,
        send_sem=send_sem,
        recv_sem=recv_sem,
        device_id=device,
        device_id_type=MESH,
    )
    copy.start()
    return copy


def one_hot(rows, cols, source):
    row = lax.broadcasted_iota(jnp.int32, (rows, cols), 0)
    col = lax.broadcasted_iota(jnp.int32, (rows, cols), 1)
    return jnp.where(col == source(row), 1.0, 0.0).astype(BF)


def compact_source(row):
    chunk, inner = row // 16, row % 16
    first = jnp.where(chunk == 0, 4, 2 * chunk - 2)
    return inner // 2 * 8 + first + inner % 2


def swapped_source(row):
    outer, inner, j = row // 16, row // 2 % 8, row % 2
    return inner * 16 + outer * 2 + j


def device_of(row):
    k, z, v = row // 128, row // 32 % 4, row // 16 % 2
    x, u = row // 4 % 4, row // 2 % 2
    return 16 * (2 * x + u) + 8 * v + 2 * z + k


def kernel(
    starts, ends, ti, qi, tg, qg, bi, bo, eig, out,
    xi, gi, ra, rb, ai, ag, bfull, pi, pg, si, sg, ri, rg, ui, ug, hi, hg,
    inverse, a_query, g_query, a_train, g_train, scaled, acc, turn, place, stage,
    ssem, rsem,
):
    x, u, v, z, k = (lax.axis_index(a) for a in ALL)
    r, p = x * 2 + u, v * 4 + z
    other = 1 - k
    y = u * 2 + v

    def row_peer(d):
        q = lax.rem(r + d, 8)
        return q, {"x": q // 2, "u": lax.rem(q, 2)}

    def col_peer(d):
        q = lax.rem(p + d, 8)
        return q, {"v": q // 4, "z": lax.rem(q, 4)}

    def x_peer(d):
        return {"x": lax.rem(x + d, 4)}

    def z_peer(d):
        return {"z": lax.rem(z + d, 4)}

    def y_peer(d):
        q = lax.rem(y + d, 4)
        return {"u": q // 2, "v": lax.rem(q, 2)}

    barrier = pltpu.get_barrier_semaphore()
    for d in range(1, 8):
        for peer in (row_peer(d)[1], col_peer(d)[1]):
            pl.semaphore_signal(barrier, inc=1, device_id=peer, device_id_type=MESH)
    pl.semaphore_signal(barrier, inc=1, device_id={"k": other}, device_id_type=MESH)
    pl.semaphore_signal(barrier, inc=1, device_id={"u": 1 - u, "v": 1 - v}, device_id_type=MESH)

    for rows, train, query in ((xi, ti, qi), (gi, tg, qg)):
        rows[...] = jnp.concatenate(
            [train[...].astype(F32), query[...].astype(F32), jnp.zeros((2, D_IN), F32)], axis=0
        ).astype(BF)
    pl.semaphore_wait(barrier, 16)

    first = []
    for d in range(1, 8):
        q, peer = row_peer(d)
        first.append(send(
            xi.at[:, pl.ds(pl.multiple_of(q * 1024, 1024), 1024)], ra.at[r],
            ssem.at[1, d], rsem.at[1, d], peer,
        ))
        q, peer = col_peer(d)
        first.append(send(
            gi.at[:, pl.ds(pl.multiple_of(q * 1024, 1024), 1024)], rb.at[2 * z + v],
            ssem.at[2, d], rsem.at[2, d], peer,
        ))
    basis_copy = send(
        bo.at[:, pl.ds(pl.multiple_of(other * 512, 512), 512)],
        bfull.at[pl.ds(pl.multiple_of(k * 512, 512), 512)],
        ssem.at[0, 0], rsem.at[0, 0], {"k": other},
    )
    ra[r] = xi[:, pl.ds(pl.multiple_of(r * 1024, 1024), 1024)]
    rb[2 * z + v] = gi[:, pl.ds(pl.multiple_of(p * 1024, 1024), 1024)]
    bfull[pl.ds(pl.multiple_of(k * 512, 512), 512), :] = bo[:, pl.ds(pl.multiple_of(k * 512, 512), 512)]
    inverse[...] = 1.0 / (eig[...] + damping)
    turn[...] = one_hot(128, 128, swapped_source)
    pick = one_hot(48, 64, compact_source)
    for copy in first:
        copy.wait()
    rows_in = jnp.dot(pick, ra[...].reshape(64, 1024), preferred_element_type=F32).astype(BF)
    rows_out = jnp.dot(pick, rb[...].reshape(64, 1024), preferred_element_type=F32).astype(BF)

    moving = {}

    def wait(c, step):
        for copy in moving.pop((c, step)):
            copy.wait()

    def sem(c, step, i):
        at = (3 + c * 8 + step, i)
        return ssem.at[at], rsem.at[at]

    def gather_y(c):
        ai[c, k, z, v] = rows_in[16 * c : 16 * c + 16]
        ag[c, k, x, u] = rows_out[16 * c : 16 * c + 16]
        moving[c, 0] = [
            send(ai.at[c, k, z, v], ai.at[c, k, z, v], *sem(c, 0, 0), {"v": 1 - v}),
            send(ag.at[c, k, x, u], ag.at[c, k, x, u], *sem(c, 0, 1), {"u": 1 - u}),
        ]

    def gather_xz(c):
        wait(c, 0)
        moving[c, 1] = []
        for d in range(1, 4):
            moving[c, 1] += [
                send(ai.at[c, k, z], ai.at[c, k, z], *sem(c, 1, d), z_peer(d)),
                send(ag.at[c, k, x], ag.at[c, k, x], *sem(c, 1, d + 3), x_peer(d)),
            ]

    def swap(c):
        wait(c, 1)
        moving[c, 2] = [
            send(ai.at[c, k], ai.at[c, k], *sem(c, 2, 0), {"k": other}),
            send(ag.at[c, k], ag.at[c, k], *sem(c, 2, 1), {"k": other}),
        ]

    def rotate(c):
        wait(c, 2)
        part = jnp.dot(ai[c].reshape(256, 1024), bi[...], preferred_element_type=F32)
        for b in range(4):
            pi[c, b] = part[:, b * 128 : (b + 1) * 128]
            si[c, b] = part[:, b * 128 : (b + 1) * 128].astype(BF)
        for h in range(2):
            lines = jnp.dot(
                turn[...], ag[c, h].reshape(128, 1024), preferred_element_type=F32
            ).astype(BF)
            part = jnp.dot(lines, bfull[...], preferred_element_type=F32)
            for b in range(4):
                pg[c, b, pl.ds(h * 128, 128)] = part[:, b * 128 : (b + 1) * 128]
                sg[c, b, pl.ds(h * 128, 128)] = part[:, b * 128 : (b + 1) * 128].astype(BF)
        moving[c, 3] = []
        for d in range(1, 4):
            q = lax.rem(x + d, 4)
            moving[c, 3].append(send(si.at[c, q], ri.at[c, d - 1], *sem(c, 3, d), {"x": q}))
            q = lax.rem(z + d, 4)
            moving[c, 3].append(send(sg.at[c, q], rg.at[c, d - 1], *sem(c, 3, d + 3), {"z": q}))

    def half_of(part, c, at, which):
        return part.at[c, at, pl.ds(pl.multiple_of(which * 128, 128), 128)]

    def reduce_y(c):
        wait(c, 3)
        for part, got, at in ((pi, ri, x), (pg, rg, z)):
            value = part[c, at]
            for d in range(3):
                value = value + got[c, d].astype(F32)
            part[c, at] = value
        moving[c, 4] = [
            send(half_of(pi, c, x, 1 - u), ui.at[c], *sem(c, 4, 0), {"u": 1 - u}),
            send(half_of(pg, c, z, 1 - v), ug.at[c], *sem(c, 4, 1), {"v": 1 - v}),
        ]

    def spread_y(c):
        wait(c, 4)
        hi[c, x, u] = (half_of(pi, c, x, u)[...] + ui[c]).astype(BF)
        hg[c, k, z, v] = (half_of(pg, c, z, v)[...] + ug[c]).astype(BF)
        moving[c, 5] = [
            send(hi.at[c, x, u], hi.at[c, x, u], *sem(c, 5, 0), {"u": 1 - u}),
            send(hg.at[c, k, z, v], hg.at[c, k, z, v], *sem(c, 5, 1), {"v": 1 - v}),
        ]

    def spread_xz(c):
        wait(c, 5)
        moving[c, 6] = []
        for d in range(1, 4):
            moving[c, 6] += [
                send(hi.at[c, x], hi.at[c, x], *sem(c, 6, d), x_peer(d)),
                send(hg.at[c, k, z], hg.at[c, k, z], *sem(c, 6, d + 3), z_peer(d)),
            ]

    def spread_core(c):
        wait(c, 6)
        moving[c, 7] = [send(hg.at[c, k], hg.at[c, k], *sem(c, 7, 0), {"k": other})]

    def lay_query():
        wait(0, 7)
        for b in range(4):
            a_query[:, pl.ds(b * 128, 128)] = hi[0, b].reshape(256, 128).astype(F32)
            for s in range(2):
                block = hg[0, s, b].reshape(256, 128).astype(F32)
                g_query[pl.ds(s * 512 + b * 128, 128), :] = jnp.transpose(block, (1, 0)).astype(BF)

    def scale(low, high):
        def body(q, carry):
            row = lax.broadcasted_iota(jnp.int32, (256, 512), 0)
            true_row = 2 * device_of(row) + row % 2
            inside = (true_row >= starts[q]) & (true_row < ends[q])
            rows = jnp.where(inside, a_query[...], 0.0).astype(BF)
            for o in range(4):
                at = pl.ds(o * 256, 256)
                outer = jnp.dot(g_query[at, :], rows, preferred_element_type=F32)
                scaled[q, at, :] = (outer * inverse[at, :]).astype(BF)
            return carry

        lax.fori_loop(low, high, body, 0)

    def pair(c):
        wait(c, 7)
        for b in range(4):
            a_train[:, pl.ds(b * 128, 128)] = hi[c, b].reshape(256, 128).astype(F32)
            for s in range(2):
                g_train[:, pl.ds(s * 512 + b * 128, 128)] = hg[c, s, b].reshape(256, 128)
        rows = pl.ds((c - 1) * 256, 256)

        def body(q, carry):
            paired = jnp.dot(g_train[...], scaled[q], preferred_element_type=F32)
            column = jnp.sum(paired * a_train[...], axis=1, keepdims=True)
            lane = lax.broadcasted_iota(jnp.int32, (256, 128), 1)
            acc[rows, :] = jnp.where(lane == q, column, acc[rows, :])
            return carry

        lax.fori_loop(0, NQ, body, 0)

    for c in range(3):
        gather_y(c)
    for c in range(3):
        gather_xz(c)

    def true_train(row):
        device, chunk, j = row // 4, row // 2 % 2, row % 2
        xu, c = device // 16, device % 16
        return chunk * 256 + c % 2 * 128 + c // 2 % 4 * 32 + c // 8 * 16 + xu * 2 + j

    place[...] = one_hot(512, 512, true_train)
    acc[...] = jnp.zeros_like(acc)
    swap(0)
    basis_copy.wait()
    rotate(0)
    swap(1)
    rotate(1)
    reduce_y(0)
    swap(2)
    rotate(2)
    spread_y(0)
    reduce_y(1)
    spread_xz(0)
    spread_y(1)
    reduce_y(2)
    spread_core(0)
    spread_xz(1)
    spread_y(2)
    lay_query()
    scale(0, 5)
    spread_xz(2)
    scale(5, 10)
    spread_core(1)
    scale(10, 16)
    spread_core(2)
    pair(1)
    pair(2)

    value, total = acc[...], 0.0
    for _ in range(3):
        piece = value.astype(BF)
        value = value - piece.astype(F32)
        total = total + jnp.dot(place[...], piece, preferred_element_type=F32)
    value = jnp.transpose(total, (1, 0))[0:NQ]
    stage[0, k] = value
    send(stage.at[0, k], stage.at[0, k], ssem.at[27, 0], rsem.at[27, 0], {"k": other}).wait()
    value = stage[0, 0] + stage[0, 1]
    for n, (at, peer) in enumerate(((z, z_peer), (x, x_peer), (y, y_peer)), 1):
        stage[n, at] = value
        copies = [
            send(stage.at[n, at], stage.at[n, at], ssem.at[27 + n, d], rsem.at[27 + n, d], peer(d))
            for d in range(1, 4)
        ]
        for copy in copies:
            copy.wait()
        value = (stage[n, 0] + stage[n, 1]) + (stage[n, 2] + stage[n, 3])
    out[...] = value * (1.0 / math.sqrt(D_IN * D_OUT * QBLOCK))


def shards(
    train_inputs,
    train_grads,
    query_inputs,
    query_grads,
    input_basis,
    output_basis,
    eigenvalues,
    query_starts,
    query_ends,
):
    vmem = pl.BlockSpec(memory_space=pltpu.VMEM)
    smem = pl.BlockSpec(memory_space=pltpu.SMEM)
    return pl.pallas_call(
        kernel,
        out_shape=jax.ShapeDtypeStruct((NQ, 512), F32),
        in_specs=[smem, smem] + [vmem] * 7,
        out_specs=vmem,
        scratch_shapes=[
            pltpu.VMEM((8, 8192), BF),
            pltpu.VMEM((8, 8192), BF),
            pltpu.VMEM((8, 8, 1024), BF),
            pltpu.VMEM((8, 8, 1024), BF),
            pltpu.VMEM((3, 2, 4, 2, 16, 1024), BF),
            pltpu.VMEM((3, 2, 4, 2, 16, 1024), BF),
            pltpu.VMEM((1024, 512), BF),
            pltpu.VMEM((3, 4, 256, 128), F32),
            pltpu.VMEM((3, 4, 256, 128), F32),
            pltpu.VMEM((3, 4, 256, 128), BF),
            pltpu.VMEM((3, 4, 256, 128), BF),
            pltpu.VMEM((3, 3, 256, 128), BF),
            pltpu.VMEM((3, 3, 256, 128), BF),
            pltpu.VMEM((3, 128, 128), F32),
            pltpu.VMEM((3, 128, 128), F32),
            pltpu.VMEM((3, 4, 2, 128, 128), BF),
            pltpu.VMEM((3, 2, 4, 2, 128, 128), BF),
            pltpu.VMEM((1024, 512), F32),
            pltpu.VMEM((256, 512), F32),
            pltpu.VMEM((1024, 256), BF),
            pltpu.VMEM((256, 512), F32),
            pltpu.VMEM((256, 1024), BF),
            pltpu.VMEM((NQ, 1024, 512), BF),
            pltpu.VMEM((512, 128), F32),
            pltpu.VMEM((128, 128), BF),
            pltpu.VMEM((512, 512), BF),
            pltpu.VMEM((4, 4, NQ, 512), F32),
            pltpu.SemaphoreType.DMA((31, 8)),
            pltpu.SemaphoreType.DMA((31, 8)),
        ],
        compiler_params=pltpu.CompilerParams(
            collective_id=0, has_side_effects=True, vmem_limit_bytes=56 * 2**20
        ),
    )(
        query_starts, query_ends, train_inputs, query_inputs, train_grads, query_grads,
        input_basis, output_basis, eigenvalues,
    )


def solution(mesh):
    split = Mesh(mesh.devices.reshape(4, 2, 2, 4, 2), ALL)
    placed = (
        P(ROW + COL, None),
        P(ROW + COL, None),
        P(ROW + COL, None),
        P(ROW + COL, None),
        P(ROW, COL),
        P(COL, ROW),
        P(ROW, COL),
        P(),
        P(),
    )
    return jax.shard_map(shards, mesh=split, in_specs=placed, out_specs=P(), check_vma=False)
```

```python
import math

import jax
import jax.numpy as jnp
from jax import lax
from jax.experimental import pallas as pl
from jax.experimental.pallas import tpu as pltpu
from jax.sharding import Mesh
from jax.sharding import PartitionSpec as P

D_IN = 8192
D_OUT = 8192
QBLOCK = 128
NQ = 16
MESH = pl.DeviceIdType.MESH
ROW = ("x", "u")
COL = ("v", "z", "k")
ALL = ("x", "u", "v", "z", "k")
damping = 0.1
BF = jnp.bfloat16
F32 = jnp.float32


def send(src, dst, send_sem, recv_sem, device):
    copy = pltpu.make_async_remote_copy(
        src_ref=src,
        dst_ref=dst,
        send_sem=send_sem,
        recv_sem=recv_sem,
        device_id=device,
        device_id_type=MESH,
    )
    copy.start()
    return copy


def one_hot(rows, cols, source):
    row = lax.broadcasted_iota(jnp.int32, (rows, 1), 0)
    col = lax.broadcasted_iota(jnp.int32, (rows, cols), 1)
    return jnp.where(col == source(row), 1.0, 0.0).astype(BF)


def compact_source(row):
    chunk, inner = row // 16, row % 16
    first = jnp.where(chunk == 0, 4, 2 * chunk - 2)
    return inner // 2 * 8 + first + inner % 2


def swapped_source(row):
    outer, inner, j = row // 16, row // 2 % 8, row % 2
    return inner * 16 + outer * 2 + j


def device_of(row):
    k, z, v = row // 128, row // 32 % 4, row // 16 % 2
    x, u = row // 4 % 4, row // 2 % 2
    return 16 * (2 * x + u) + 8 * v + 2 * z + k


def turned(block):
    return jnp.transpose(block.astype(F32), (1, 0))


def kernel(
    starts, ends, ti, qi, tg, qg, bi_hbm, bo_hbm, eig_hbm, out,
    tiv, qiv, tgv, qgv, bi, bo, eig,
    xi, gi, ra, rb, ai, ag, bfull, pi, pg, si, sg, ri, rg, yqi, yqg, yti, ytg, wti, wtg, hi, hg,
    inverse, a_query, g_query, a_train, g_train, scaled, acc, turn, place, true_rows, stage,
    lsem, ssem, rsem,
):
    x, u, v, z, k = (lax.axis_index(a) for a in ALL)
    r, p = x * 2 + u, v * 4 + z
    other = 1 - k
    y = u * 2 + v

    def row_peer(d):
        q = lax.rem(r + d, 8)
        return q, {"x": q // 2, "u": lax.rem(q, 2)}

    def col_peer(d):
        q = lax.rem(p + d, 8)
        return q, {"v": q // 4, "z": lax.rem(q, 4)}

    def x_peer(d):
        return {"x": lax.rem(x + d, 4)}

    def z_peer(d):
        return {"z": lax.rem(z + d, 4)}

    def y_peer(d):
        q = lax.rem(y + d, 4)
        return {"u": q // 2, "v": lax.rem(q, 2)}

    barrier = pltpu.get_barrier_semaphore()
    for d in range(1, 8):
        for peer in (row_peer(d)[1], col_peer(d)[1]):
            pl.semaphore_signal(barrier, inc=1, device_id=peer, device_id_type=MESH)
    pl.semaphore_signal(barrier, inc=1, device_id={"k": other}, device_id_type=MESH)
    pl.semaphore_signal(barrier, inc=1, device_id={"u": 1 - u, "v": 1 - v}, device_id_type=MESH)

    local = []
    for i, (src, dst) in enumerate((
        (ti, tiv), (qi, qiv), (tg, tgv), (qg, qgv), (bo_hbm, bo), (bi_hbm, bi), (eig_hbm, eig)
    )):
        local.append(pltpu.make_async_copy(src, dst, lsem.at[i]))
        local[-1].start()
    for copy in local[:4]:
        copy.wait()
    for rows, train, query in ((xi, tiv, qiv), (gi, tgv, qgv)):
        rows[...] = jnp.concatenate(
            [train[...].astype(F32), query[...].astype(F32), jnp.zeros((2, D_IN), F32)], axis=0
        ).astype(BF)
    pl.semaphore_wait(barrier, 16)

    first = ([], [])
    for d in range(1, 8):
        q, peer = row_peer(d)
        first[0].append(send(
            xi.at[:, pl.ds(pl.multiple_of(q * 1024, 1024), 1024)], ra.at[r],
            ssem.at[1, d], rsem.at[1, d], peer,
        ))
        q, peer = col_peer(d)
        first[1].append(send(
            gi.at[:, pl.ds(pl.multiple_of(q * 1024, 1024), 1024)], rb.at[2 * z + v],
            ssem.at[2, d], rsem.at[2, d], peer,
        ))
    ra[r] = xi[:, pl.ds(pl.multiple_of(r * 1024, 1024), 1024)]
    rb[2 * z + v] = gi[:, pl.ds(pl.multiple_of(p * 1024, 1024), 1024)]
    pick = one_hot(48, 64, compact_source)
    local[4].wait()
    basis_copy = send(
        bo.at[:, pl.ds(pl.multiple_of(other * 512, 512), 512)],
        bfull.at[pl.ds(pl.multiple_of(k * 512, 512), 512)],
        ssem.at[0, 0], rsem.at[0, 0], {"k": other},
    )
    turn[...] = one_hot(128, 128, swapped_source)
    lanes = lax.broadcasted_iota(jnp.int32, (1, 256), 1)
    true_rows[...] = 2 * device_of(lanes) + lanes % 2

    moving = {}

    def wait(*key):
        for copy in moving.pop(key):
            copy.wait()

    def sems(side, c, step, i):
        at = (3 + side * 18 + c * 6 + step, i)
        return ssem.at[at], rsem.at[at]

    gathered = (ai, ag)
    gather_at = ((z, v), (x, u))
    gather_y_peer = ({"v": 1 - v}, {"u": 1 - u})
    gather_peer = (z_peer, x_peer)
    sum_at = (x, z)
    sum_name = ("x", "z")
    sum_y_peer = ({"u": 1 - u}, {"v": 1 - v})
    part = (pi, pg)
    small = (si, sg)
    got = (ri, rg)
    wide_y = (yqi, yqg)
    mine_y = (wti, wtg)
    their_y = (yti, ytg)

    def gather_y(side, rows):
        at = gather_at[side]
        for c in range(3):
            ref = gathered[side].at[c, k, at[0], at[1]]
            ref[...] = rows[16 * c : 16 * c + 16]
            moving[side, c, 0] = [send(ref, ref, *sems(side, c, 0, 0), gather_y_peer[side])]

    def gather_xz(side, c):
        wait(side, c, 0)
        ref = gathered[side].at[c, k, gather_at[side][0]]
        moving[side, c, 1] = [
            send(ref, ref, *sems(side, c, 1, d), gather_peer[side](d)) for d in range(1, 4)
        ]

    def swap(c):
        for side in range(2):
            wait(side, c, 1)
            ref = gathered[side].at[c, k]
            moving[side, c, 2] = [send(ref, ref, *sems(side, c, 2, 0), {"k": other})]

    def rotate(c):
        for side in range(2):
            wait(side, c, 2)
            if side == 0:
                blocks = [(0, 256, ai[c].reshape(256, 1024), bi)]
            else:
                blocks = [
                    (h * 128, 128, jnp.dot(
                        turn[...], ag[c, h].reshape(128, 1024), preferred_element_type=F32
                    ).astype(BF), bfull)
                    for h in range(2)
                ]
            for low, size, rows, basis in blocks:
                value = jnp.dot(rows, basis[...], preferred_element_type=F32)
                for b in range(4):
                    piece = value[:, b * 128 : (b + 1) * 128]
                    part[side][c, b, pl.ds(low, size)] = piece
                    small[side][c, b, pl.ds(low, size)] = piece.astype(BF)
            moving[side, c, 3] = []
            for d in range(1, 4):
                q = lax.rem(sum_at[side] + d, 4)
                moving[side, c, 3].append(send(
                    small[side].at[c, q], got[side].at[c, d - 1], *sems(side, c, 3, d),
                    {sum_name[side]: q},
                ))

    def reduce_y(c):
        for side in range(2):
            wait(side, c, 3)
            at = sum_at[side]
            value = part[side][c, at]
            for d in range(3):
                value = value + got[side][c, d].astype(F32)
            part[side][c, at] = value
            if c == 0:
                src, dst = part[side].at[c, at], wide_y[side]
            else:
                mine_y[side][c - 1] = value.astype(BF)
                src, dst = mine_y[side].at[c - 1], their_y[side].at[c - 1]
            moving[side, c, 4] = [send(src, dst, *sems(side, c, 4, 0), sum_y_peer[side])]

    def spread(c):
        for side in range(2):
            wait(side, c, 4)
            at = sum_at[side]
            more = wide_y[side][...] if c == 0 else their_y[side][c - 1].astype(F32)
            ref = hi.at[c, at] if side == 0 else hg.at[c, k, at]
            ref[...] = (part[side][c, at] + more).astype(BF)
            peer = x_peer if side == 0 else z_peer
            moving[side, c, 5] = [
                send(ref, ref, *sems(side, c, 5, d), peer(d)) for d in range(1, 4)
            ]

    def spread_core(c):
        wait(1, c, 5)
        moving[1, c, 6] = [send(hg.at[c, k], hg.at[c, k], *sems(0, c, 5, 6), {"k": other})]

    def lay_query():
        wait(0, 0, 5)
        for b in range(4):
            a_query[pl.ds(b * 128, 128), :] = turned(hi[0, b])
        wait(1, 0, 6)
        for b in range(4):
            for s in range(2):
                g_query[:, pl.ds(s * 512 + b * 128, 128)] = hg[0, s, b]

    def scale(low, high):
        def body(q, carry):
            inside = (true_rows[...] >= starts[q]) & (true_rows[...] < ends[q])
            rows = jnp.where(inside, a_query[...], 0.0).astype(BF)
            for o in range(4):
                at = pl.ds(o * 256, 256)
                outer = jnp.dot(rows, g_query[:, at], preferred_element_type=F32)
                scaled[q, :, at] = (outer * inverse[:, at]).astype(BF)
            return carry

        lax.fori_loop(low, high, body, 0, unroll=high - low)

    def lay_train(c):
        wait(0, c, 5)
        for b in range(4):
            a_train[c - 1, pl.ds(b * 128, 128), :] = turned(hi[c, b])
        wait(1, c, 6)
        for b in range(4):
            for s in range(2):
                g_train[c - 1, pl.ds(s * 512 + b * 128, 128), :] = turned(hg[c, s, b]).astype(BF)

    def pair(c, low, high):
        def body(q, carry):
            paired = jnp.dot(scaled[q], g_train[c - 1], preferred_element_type=F32)
            acc[c - 1, pl.ds(q, 1), :] = jnp.sum(paired * a_train[c - 1], axis=0, keepdims=True)
            return carry

        lax.fori_loop(low, high, body, 0, unroll=high - low)

    score_at = (k, z, x, y)
    score_peer = (lambda d: {"k": other}, z_peer, x_peer, y_peer)

    def share(half, n):
        if n == 0:
            value = acc[half]
        else:
            value = summed(half, n - 1)
        stage[half, n, score_at[n]] = value
        ref = stage.at[half, n, score_at[n]]
        moving[half, n] = [
            send(ref, ref, ssem.at[39 + half * 4 + n, d], rsem.at[39 + half * 4 + n, d], score_peer[n](d))
            for d in range(1, 2 if n == 0 else 4)
        ]

    def summed(half, n):
        wait(half, n)
        value = stage[half, n, 0] + stage[half, n, 1]
        if n:
            value = value + (stage[half, n, 2] + stage[half, n, 3])
        return value

    def in_order(value, half):
        total = 0.0
        for _ in range(3):
            piece = value.astype(BF)
            value = value - piece.astype(F32)
            total = total + jnp.dot(piece, place[half], preferred_element_type=F32)
        return total

    for side, rows in ((0, ra), (1, rb)):
        for copy in first[side]:
            copy.wait()
        gather_y(side, jnp.dot(pick, rows[...].reshape(64, 1024), preferred_element_type=F32).astype(BF))
    bfull[pl.ds(pl.multiple_of(k * 512, 512), 512), :] = bo[:, pl.ds(pl.multiple_of(k * 512, 512), 512)]
    for c in range(3):
        for side in range(2):
            gather_xz(side, c)

    train = lax.broadcasted_iota(jnp.int32, (1, 512), 1)
    device = train // 4
    spot = train // 2 % 2 * 256 + device % 2 * 128 + device // 2 % 4 * 32 + device % 16 // 8 * 16
    spot = spot + device // 16 * 2 + train % 2
    row = lax.broadcasted_iota(jnp.int32, (512, 512), 0)
    place[...] = jnp.where(row == spot, 1.0, 0.0).astype(BF).reshape(2, 256, 512)
    local[5].wait()
    basis_copy.wait()
    swap(0)
    rotate(0)
    swap(1)
    rotate(1)
    swap(2)
    rotate(2)
    local[6].wait()
    inverse[...] = jnp.transpose(1.0 / (eig[...] + damping), (1, 0))
    reduce_y(0)
    reduce_y(1)
    spread(0)
    reduce_y(2)
    spread(1)
    spread(2)
    spread_core(0)
    lay_query()
    scale(0, 8)
    spread_core(1)
    spread_core(2)
    scale(8, 16)
    lay_train(1)
    pair(1, 0, 16)
    share(0, 0)
    lay_train(2)
    pair(2, 0, 8)
    share(0, 1)
    pair(2, 8, 16)
    share(1, 0)
    share(0, 2)
    share(1, 1)
    share(0, 3)
    share(1, 2)
    early = in_order(summed(0, 3), 0)
    share(1, 3)
    total = early + in_order(summed(1, 3), 1)
    out[...] = total * (1.0 / math.sqrt(D_IN * D_OUT * QBLOCK))


def shards(
    train_inputs,
    train_grads,
    query_inputs,
    query_grads,
    input_basis,
    output_basis,
    eigenvalues,
    query_starts,
    query_ends,
):
    vmem = pl.BlockSpec(memory_space=pltpu.VMEM)
    smem = pl.BlockSpec(memory_space=pltpu.SMEM)
    return pl.pallas_call(
        kernel,
        out_shape=jax.ShapeDtypeStruct((NQ, 512), F32),
        in_specs=[smem, smem] + [pl.BlockSpec(memory_space=pl.ANY)] * 7,
        out_specs=vmem,
        scratch_shapes=[
            pltpu.VMEM((4, 8192), BF),
            pltpu.VMEM((2, 8192), BF),
            pltpu.VMEM((4, 8192), BF),
            pltpu.VMEM((2, 8192), BF),
            pltpu.VMEM((1024, 512), BF),
            pltpu.VMEM((512, 1024), BF),
            pltpu.VMEM((1024, 512), F32),
            pltpu.VMEM((8, 8192), BF),
            pltpu.VMEM((8, 8192), BF),
            pltpu.VMEM((8, 8, 1024), BF),
            pltpu.VMEM((8, 8, 1024), BF),
            pltpu.VMEM((3, 2, 4, 2, 16, 1024), BF),
            pltpu.VMEM((3, 2, 4, 2, 16, 1024), BF),
            pltpu.VMEM((1024, 512), BF),
            pltpu.VMEM((3, 4, 256, 128), F32),
            pltpu.VMEM((3, 4, 256, 128), F32),
            pltpu.VMEM((3, 4, 256, 128), BF),
            pltpu.VMEM((3, 4, 256, 128), BF),
            pltpu.VMEM((3, 3, 256, 128), BF),
            pltpu.VMEM((3, 3, 256, 128), BF),
            pltpu.VMEM((256, 128), F32),
            pltpu.VMEM((256, 128), F32),
            pltpu.VMEM((2, 256, 128), BF),
            pltpu.VMEM((2, 256, 128), BF),
            pltpu.VMEM((2, 256, 128), BF),
            pltpu.VMEM((2, 256, 128), BF),
            pltpu.VMEM((3, 4, 256, 128), BF),
            pltpu.VMEM((3, 2, 4, 256, 128), BF),
            pltpu.VMEM((512, 1024), F32),
            pltpu.VMEM((512, 256), F32),
            pltpu.VMEM((256, 1024), BF),
            pltpu.VMEM((2, 512, 256), F32),
            pltpu.VMEM((2, 1024, 256), BF),
            pltpu.VMEM((NQ, 512, 1024), BF),
            pltpu.VMEM((2, NQ, 256), F32),
            pltpu.VMEM((128, 128), BF),
            pltpu.VMEM((2, 256, 512), BF),
            pltpu.VMEM((1, 256), jnp.int32),
            pltpu.VMEM((2, 4, 4, NQ, 256), F32),
            pltpu.SemaphoreType.DMA((7,)),
            pltpu.SemaphoreType.DMA((47, 8)),
            pltpu.SemaphoreType.DMA((47, 8)),
        ],
        compiler_params=pltpu.CompilerParams(
            collective_id=0, has_side_effects=True, vmem_limit_bytes=56 * 2**20
        ),
    )(
        query_starts, query_ends, train_inputs, query_inputs, train_grads, query_grads,
        input_basis, output_basis, eigenvalues,
    )


def solution(mesh):
    split = Mesh(mesh.devices.reshape(4, 2, 2, 4, 2), ALL)
    placed = (
        P(ROW + COL, None),
        P(ROW + COL, None),
        P(ROW + COL, None),
        P(ROW + COL, None),
        P(ROW, COL),
        P(COL, ROW),
        P(ROW, COL),
        P(),
        P(),
    )
    return jax.shard_map(shards, mesh=split, in_specs=placed, out_specs=P(), check_vma=False)
```

```python
import math

import jax
import jax.numpy as jnp
from jax import lax
from jax.experimental import pallas as pl
from jax.experimental.pallas import tpu as pltpu
from jax.sharding import Mesh
from jax.sharding import PartitionSpec as P

D_IN = 8192
D_OUT = 8192
QBLOCK = 128
NQ = 16
MESH = pl.DeviceIdType.MESH
ROW = ("x", "u")
COL = ("v", "z", "k")
ALL = ("x", "u", "v", "z", "k")
damping = 0.1
BF = jnp.bfloat16
F32 = jnp.float32


def send(src, dst, send_sem, recv_sem, device):
    copy = pltpu.make_async_remote_copy(
        src_ref=src,
        dst_ref=dst,
        send_sem=send_sem,
        recv_sem=recv_sem,
        device_id=device,
        device_id_type=MESH,
    )
    copy.start()
    return copy


def arrival(ref, send_sem, recv_sem, device):
    return pltpu.make_async_remote_copy(
        src_ref=ref,
        dst_ref=ref,
        send_sem=send_sem,
        recv_sem=recv_sem,
        device_id=device,
        device_id_type=MESH,
    )


def one_hot(rows, cols, source):
    row = lax.broadcasted_iota(jnp.int32, (rows, 1), 0)
    col = lax.broadcasted_iota(jnp.int32, (rows, cols), 1)
    return jnp.where(col == source(row), 1.0, 0.0).astype(BF)


def compact_source(row):
    chunk, inner = row // 16, row % 16
    first = jnp.where(chunk == 0, 4, 2 * chunk - 2)
    return inner // 2 * 8 + first + inner % 2


def swapped_source(row):
    outer, inner, j = row // 16, row // 2 % 8, row % 2
    return inner * 16 + outer * 2 + j


def device_of(row):
    k, z, v = row // 128, row // 32 % 4, row // 16 % 2
    x, u = row // 4 % 4, row // 2 % 2
    return 16 * (2 * x + u) + 8 * v + 2 * z + k


def turned(block):
    return jnp.transpose(block.astype(F32), (1, 0))


def kernel(
    starts, ends, ti, qi, tg, qg, bi_hbm, bo_hbm, eig_hbm, out,
    tiv, qiv, tgv, qgv, bi, bo, eig,
    xi, gi, ra, rb, ai, ag, bfull, pi, pg, si, sg, ri, rg, yqi, yqg, yti, ytg, wti, wtg, hi, hg,
    inverse, a_query, g_query, a_train, g_train, scaled, acc, turn, place, true_rows, stage,
    lsem, ssem, rsem,
):
    x, u, v, z, k = (lax.axis_index(a) for a in ALL)
    r, p = x * 2 + u, v * 4 + z
    other = 1 - k
    y = u * 2 + v

    def row_peer(d):
        q = lax.rem(r + d, 8)
        return q, {"x": q // 2, "u": lax.rem(q, 2)}

    def col_peer(d):
        q = lax.rem(p + d, 8)
        return q, {"v": q // 4, "z": lax.rem(q, 4)}

    def x_peer(d):
        return {"x": lax.rem(x + d, 4)}

    def z_peer(d):
        return {"z": lax.rem(z + d, 4)}

    def y_peer(d):
        q = lax.rem(y + d, 4)
        return {"u": q // 2, "v": lax.rem(q, 2)}

    barrier = pltpu.get_barrier_semaphore()
    for d in range(1, 8):
        for peer in (row_peer(d)[1], col_peer(d)[1]):
            pl.semaphore_signal(barrier, inc=1, device_id=peer, device_id_type=MESH)
    pl.semaphore_signal(barrier, inc=1, device_id={"k": other}, device_id_type=MESH)
    pl.semaphore_signal(barrier, inc=1, device_id={"u": 1 - u, "v": 1 - v}, device_id_type=MESH)

    local = []
    for i, (src, dst) in enumerate((
        (ti, tiv), (qi, qiv), (tg, tgv), (qg, qgv), (bo_hbm, bo), (bi_hbm, bi), (eig_hbm, eig)
    )):
        local.append(pltpu.make_async_copy(src, dst, lsem.at[i]))
        local[-1].start()
    for copy in local[:4]:
        copy.wait()
    for rows, train, query in ((xi, tiv, qiv), (gi, tgv, qgv)):
        rows[...] = jnp.concatenate(
            [train[...].astype(F32), query[...].astype(F32), jnp.zeros((2, D_IN), F32)], axis=0
        ).astype(BF)
    pl.semaphore_wait(barrier, 16)

    for d in range(1, 8):
        q, peer = row_peer(d)
        send(
            xi.at[:, pl.ds(pl.multiple_of(q * 1024, 1024), 1024)], ra.at[r],
            ssem.at[1], rsem.at[1], peer,
        )
        q, peer = col_peer(d)
        send(
            gi.at[:, pl.ds(pl.multiple_of(q * 1024, 1024), 1024)], rb.at[2 * z + v],
            ssem.at[2], rsem.at[2], peer,
        )
    first = (
        arrival(ra.at[0:7], ssem.at[1], rsem.at[1], row_peer(1)[1]),
        arrival(rb.at[0:7], ssem.at[2], rsem.at[2], col_peer(1)[1]),
    )
    ra[r] = xi[:, pl.ds(pl.multiple_of(r * 1024, 1024), 1024)]
    rb[2 * z + v] = gi[:, pl.ds(pl.multiple_of(p * 1024, 1024), 1024)]
    pick = one_hot(48, 64, compact_source)
    local[4].wait()
    basis_copy = send(
        bo.at[:, pl.ds(pl.multiple_of(other * 512, 512), 512)],
        bfull.at[pl.ds(pl.multiple_of(k * 512, 512), 512)],
        ssem.at[0], rsem.at[0], {"k": other},
    )
    turn[...] = one_hot(128, 128, swapped_source)
    lanes = lax.broadcasted_iota(jnp.int32, (1, 256), 1)
    true_rows[...] = 2 * device_of(lanes) + lanes % 2

    moving = {}

    def wait(*key):
        moving.pop(key).wait()

    def sems(side, c, step):
        return ssem.at[3 + side * 3 + c], rsem.at[3 + (side * 3 + c) * 7 + step]

    gathered = (ai, ag)
    gather_at = ((z, v), (x, u))
    gather_y_peer = ({"v": 1 - v}, {"u": 1 - u})
    gather_peer = (z_peer, x_peer)
    sum_at = (x, z)
    sum_name = ("x", "z")
    sum_y_peer = ({"u": 1 - u}, {"v": 1 - v})
    part = (pi, pg)
    small = (si, sg)
    got = (ri, rg)
    wide_y = (yqi, yqg)
    mine_y = (wti, wtg)
    their_y = (yti, ytg)

    def gather_y(side, rows):
        at = gather_at[side]
        for c in range(3):
            ref = gathered[side].at[c, k, at[0], at[1]]
            ref[...] = rows[16 * c : 16 * c + 16]
            moving[side, c, 0] = send(ref, ref, *sems(side, c, 0), gather_y_peer[side])

    def gather_xz(side, c):
        wait(side, c, 0)
        ref = gathered[side].at[c, k, gather_at[side][0]]
        for d in range(1, 4):
            send(ref, ref, *sems(side, c, 1), gather_peer[side](d))
        moving[side, c, 1] = arrival(
            gathered[side].at[c, k, 0:3], *sems(side, c, 1), gather_peer[side](1)
        )

    def swap(c):
        for side in range(2):
            wait(side, c, 1)
            ref = gathered[side].at[c, k]
            moving[side, c, 2] = send(ref, ref, *sems(side, c, 2), {"k": other})

    def rotate(c):
        for side in range(2):
            wait(side, c, 2)
            if side == 0:
                blocks = [(0, 256, ai[c].reshape(256, 1024), bi)]
            else:
                blocks = [
                    (h * 128, 128, jnp.dot(
                        turn[...], ag[c, h].reshape(128, 1024), preferred_element_type=F32
                    ).astype(BF), bfull)
                    for h in range(2)
                ]
            for low, size, rows, basis in blocks:
                value = jnp.dot(rows, basis[...], preferred_element_type=F32)
                for b in range(4):
                    piece = value[:, b * 128 : (b + 1) * 128]
                    part[side][c, b, pl.ds(low, size)] = piece
                    small[side][c, b, pl.ds(low, size)] = piece.astype(BF)
            for d in range(1, 4):
                q = lax.rem(sum_at[side] + d, 4)
                send(
                    small[side].at[c, q], got[side].at[c, d - 1], *sems(side, c, 3),
                    {sum_name[side]: q},
                )
            moving[side, c, 3] = arrival(got[side].at[c], *sems(side, c, 3), {sum_name[side]: q})

    def reduce_y(c):
        for side in range(2):
            wait(side, c, 3)
            at = sum_at[side]
            value = part[side][c, at]
            for d in range(3):
                value = value + got[side][c, d].astype(F32)
            part[side][c, at] = value
            if c == 0:
                src, dst = part[side].at[c, at], wide_y[side]
            else:
                mine_y[side][c - 1] = value.astype(BF)
                src, dst = mine_y[side].at[c - 1], their_y[side].at[c - 1]
            moving[side, c, 4] = send(src, dst, *sems(side, c, 4), sum_y_peer[side])

    def spread(c):
        for side in range(2):
            wait(side, c, 4)
            at = sum_at[side]
            more = wide_y[side][...] if c == 0 else their_y[side][c - 1].astype(F32)
            ref = hi.at[c, at] if side == 0 else hg.at[c, k, at]
            ref[...] = (part[side][c, at] + more).astype(BF)
            peer = x_peer if side == 0 else z_peer
            for d in range(1, 4):
                send(ref, ref, *sems(side, c, 5), peer(d))
            three = hi.at[c, 0:3] if side == 0 else hg.at[c, k, 0:3]
            moving[side, c, 5] = arrival(three, *sems(side, c, 5), peer(1))

    def spread_core(c):
        wait(1, c, 5)
        moving[1, c, 6] = send(hg.at[c, k], hg.at[c, k], *sems(1, c, 6), {"k": other})

    def lay_query():
        wait(0, 0, 5)
        for b in range(4):
            a_query[pl.ds(b * 128, 128), :] = turned(hi[0, b])
        wait(1, 0, 6)
        for b in range(4):
            for s in range(2):
                g_query[:, pl.ds(s * 512 + b * 128, 128)] = hg[0, s, b]

    def scale(low, high):
        def body(q, carry):
            inside = (true_rows[...] >= starts[q]) & (true_rows[...] < ends[q])
            rows = jnp.where(inside, a_query[...], 0.0).astype(BF)
            for o in range(4):
                at = pl.ds(o * 256, 256)
                outer = jnp.dot(rows, g_query[:, at], preferred_element_type=F32)
                scaled[q, :, at] = (outer * inverse[:, at]).astype(BF)
            return carry

        lax.fori_loop(low, high, body, 0, unroll=high - low)

    def lay_train(c):
        wait(0, c, 5)
        for b in range(4):
            a_train[c - 1, pl.ds(b * 128, 128), :] = turned(hi[c, b])
        wait(1, c, 6)
        for b in range(4):
            for s in range(2):
                g_train[c - 1, pl.ds(s * 512 + b * 128, 128), :] = turned(hg[c, s, b]).astype(BF)

    def pair(c, low, high):
        def body(q, carry):
            paired = jnp.dot(scaled[q], g_train[c - 1], preferred_element_type=F32)
            acc[c - 1, pl.ds(q, 1), :] = jnp.sum(paired * a_train[c - 1], axis=0, keepdims=True)
            return carry

        lax.fori_loop(low, high, body, 0, unroll=high - low)

    score_at = (k, z, x, y)
    score_peer = (lambda d: {"k": other}, z_peer, x_peer, y_peer)

    def share(half, n):
        if n == 0:
            value = acc[half]
        else:
            value = summed(half, n - 1)
        stage[half, n, score_at[n]] = value
        ref = stage.at[half, n, score_at[n]]
        pair_of = (ssem.at[9 + half], rsem.at[45 + half * 4 + n])
        if n == 0:
            moving[half, n] = send(ref, ref, *pair_of, score_peer[n](1))
        else:
            for d in range(1, 4):
                send(ref, ref, *pair_of, score_peer[n](d))
            moving[half, n] = arrival(stage.at[half, n, 0:3], *pair_of, score_peer[n](1))

    def summed(half, n):
        wait(half, n)
        value = stage[half, n, 0] + stage[half, n, 1]
        if n:
            value = value + (stage[half, n, 2] + stage[half, n, 3])
        return value

    def in_order(value, half):
        total = 0.0
        for _ in range(3):
            piece = value.astype(BF)
            value = value - piece.astype(F32)
            total = total + jnp.dot(piece, place[half], preferred_element_type=F32)
        return total

    for side, rows in ((0, ra), (1, rb)):
        first[side].wait()
        gather_y(side, jnp.dot(pick, rows[...].reshape(64, 1024), preferred_element_type=F32).astype(BF))
    bfull[pl.ds(pl.multiple_of(k * 512, 512), 512), :] = bo[:, pl.ds(pl.multiple_of(k * 512, 512), 512)]
    for c in range(3):
        for side in range(2):
            gather_xz(side, c)

    train = lax.broadcasted_iota(jnp.int32, (1, 512), 1)
    device = train // 4
    spot = train // 2 % 2 * 256 + device % 2 * 128 + device // 2 % 4 * 32 + device % 16 // 8 * 16
    spot = spot + device // 16 * 2 + train % 2
    row = lax.broadcasted_iota(jnp.int32, (512, 512), 0)
    place[...] = jnp.where(row == spot, 1.0, 0.0).astype(BF).reshape(2, 256, 512)
    local[5].wait()
    basis_copy.wait()
    swap(0)
    rotate(0)
    swap(1)
    rotate(1)
    swap(2)
    rotate(2)
    local[6].wait()
    inverse[...] = jnp.transpose(1.0 / (eig[...] + damping), (1, 0))
    reduce_y(0)
    reduce_y(1)
    spread(0)
    reduce_y(2)
    spread(1)
    spread(2)
    spread_core(0)
    lay_query()
    scale(0, 8)
    spread_core(1)
    spread_core(2)
    scale(8, 16)
    lay_train(1)
    pair(1, 0, 16)
    share(0, 0)
    lay_train(2)
    pair(2, 0, 8)
    share(0, 1)
    pair(2, 8, 16)
    share(1, 0)
    share(0, 2)
    share(1, 1)
    share(0, 3)
    share(1, 2)
    early = in_order(summed(0, 3), 0)
    share(1, 3)
    total = early + in_order(summed(1, 3), 1)
    out[...] = total * (1.0 / math.sqrt(D_IN * D_OUT * QBLOCK))


def shards(
    train_inputs,
    train_grads,
    query_inputs,
    query_grads,
    input_basis,
    output_basis,
    eigenvalues,
    query_starts,
    query_ends,
):
    vmem = pl.BlockSpec(memory_space=pltpu.VMEM)
    smem = pl.BlockSpec(memory_space=pltpu.SMEM)
    return pl.pallas_call(
        kernel,
        out_shape=jax.ShapeDtypeStruct((NQ, 512), F32),
        in_specs=[smem, smem] + [pl.BlockSpec(memory_space=pl.ANY)] * 7,
        out_specs=vmem,
        scratch_shapes=[
            pltpu.VMEM((4, 8192), BF),
            pltpu.VMEM((2, 8192), BF),
            pltpu.VMEM((4, 8192), BF),
            pltpu.VMEM((2, 8192), BF),
            pltpu.VMEM((1024, 512), BF),
            pltpu.VMEM((512, 1024), BF),
            pltpu.VMEM((1024, 512), F32),
            pltpu.VMEM((8, 8192), BF),
            pltpu.VMEM((8, 8192), BF),
            pltpu.VMEM((8, 8, 1024), BF),
            pltpu.VMEM((8, 8, 1024), BF),
            pltpu.VMEM((3, 2, 4, 2, 16, 1024), BF),
            pltpu.VMEM((3, 2, 4, 2, 16, 1024), BF),
            pltpu.VMEM((1024, 512), BF),
            pltpu.VMEM((3, 4, 256, 128), F32),
            pltpu.VMEM((3, 4, 256, 128), F32),
            pltpu.VMEM((3, 4, 256, 128), BF),
            pltpu.VMEM((3, 4, 256, 128), BF),
            pltpu.VMEM((3, 3, 256, 128), BF),
            pltpu.VMEM((3, 3, 256, 128), BF),
            pltpu.VMEM((256, 128), F32),
            pltpu.VMEM((256, 128), F32),
            pltpu.VMEM((2, 256, 128), BF),
            pltpu.VMEM((2, 256, 128), BF),
            pltpu.VMEM((2, 256, 128), BF),
            pltpu.VMEM((2, 256, 128), BF),
            pltpu.VMEM((3, 4, 256, 128), BF),
            pltpu.VMEM((3, 2, 4, 256, 128), BF),
            pltpu.VMEM((512, 1024), F32),
            pltpu.VMEM((512, 256), F32),
            pltpu.VMEM((256, 1024), BF),
            pltpu.VMEM((2, 512, 256), F32),
            pltpu.VMEM((2, 1024, 256), BF),
            pltpu.VMEM((NQ, 512, 1024), BF),
            pltpu.VMEM((2, NQ, 256), F32),
            pltpu.VMEM((128, 128), BF),
            pltpu.VMEM((2, 256, 512), BF),
            pltpu.VMEM((1, 256), jnp.int32),
            pltpu.VMEM((2, 4, 4, NQ, 256), F32),
            pltpu.SemaphoreType.DMA((7,)),
            pltpu.SemaphoreType.DMA((11,)),
            pltpu.SemaphoreType.DMA((53,)),
        ],
        compiler_params=pltpu.CompilerParams(
            collective_id=0, has_side_effects=True, vmem_limit_bytes=56 * 2**20
        ),
    )(
        query_starts, query_ends, train_inputs, query_inputs, train_grads, query_grads,
        input_basis, output_basis, eigenvalues,
    )


def solution(mesh):
    split = Mesh(mesh.devices.reshape(4, 2, 2, 4, 2), ALL)
    placed = (
        P(ROW + COL, None),
        P(ROW + COL, None),
        P(ROW + COL, None),
        P(ROW + COL, None),
        P(ROW, COL),
        P(COL, ROW),
        P(ROW, COL),
        P(),
        P(),
    )
    return jax.shard_map(shards, mesh=split, in_specs=placed, out_specs=P(), check_vma=False)
```

```python
import math

import jax
import jax.numpy as jnp
from jax import lax
from jax.experimental import pallas as pl
from jax.experimental.pallas import tpu as pltpu
from jax.sharding import Mesh
from jax.sharding import PartitionSpec as P

D_IN = 8192
D_OUT = 8192
QBLOCK = 128
NQ = 16
MESH = pl.DeviceIdType.MESH
ROW = ("x", "u")
COL = ("v", "z", "k")
ALL = ("x", "u", "v", "z", "k")
damping = 0.1
BF = jnp.bfloat16
F32 = jnp.float32


def send(src, dst, send_sem, recv_sem, device):
    copy = pltpu.make_async_remote_copy(
        src_ref=src,
        dst_ref=dst,
        send_sem=send_sem,
        recv_sem=recv_sem,
        device_id=device,
        device_id_type=MESH,
    )
    copy.start()
    return copy


def arrival(ref, send_sem, recv_sem, device):
    return pltpu.make_async_remote_copy(
        src_ref=ref,
        dst_ref=ref,
        send_sem=send_sem,
        recv_sem=recv_sem,
        device_id=device,
        device_id_type=MESH,
    )


def one_hot(rows, cols, source):
    row = lax.broadcasted_iota(jnp.int32, (rows, 1), 0)
    col = lax.broadcasted_iota(jnp.int32, (rows, cols), 1)
    return jnp.where(col == source(row), 1.0, 0.0).astype(BF)


def compact_source(row):
    chunk, inner = row // 16, row % 16
    first = jnp.where(chunk == 0, 4, 2 * chunk - 2)
    return inner // 2 * 8 + first + inner % 2


def swapped_source(row):
    outer, inner, j = row // 16, row // 2 % 8, row % 2
    return inner * 16 + outer * 2 + j


def device_of(row):
    k, z, v = row // 128, row // 32 % 4, row // 16 % 2
    x, u = row // 4 % 4, row // 2 % 2
    return 16 * (2 * x + u) + 8 * v + 2 * z + k


def tree(values):
    while len(values) > 1:
        values = [a + b for a, b in zip(values[::2], values[1::2])]
    return values[0]


def turned(block):
    return jnp.transpose(block.astype(F32), (1, 0))


def kernel(
    starts, ends, ti, qi, tg, qg, bi_hbm, bo_hbm, eig_hbm, out,
    tiv, qiv, tgv, qgv, bi, bo, eig,
    xi, gi, ra, rb, ai, ag, bfull, pi, pg, si, sg, ri, rg, yqi, yqg, yti, ytg, wti, wtg, hi, hg,
    inverse, a_query, g_query, a_train, g_train, scaled, acc, turn, place, true_rows, near_sums, plane_sums,
    lsem, ssem, rsem,
):
    x, u, v, z, k = (lax.axis_index(a) for a in ALL)
    r, p = x * 2 + u, v * 4 + z
    other = 1 - k
    near, plane = u * 4 + v * 2 + k, x * 4 + z

    def row_peer(d):
        q = lax.rem(r + d, 8)
        return q, {"x": q // 2, "u": lax.rem(q, 2)}

    def col_peer(d):
        q = lax.rem(p + d, 8)
        return q, {"v": q // 4, "z": lax.rem(q, 4)}

    def x_peer(d):
        return {"x": lax.rem(x + d, 4)}

    def z_peer(d):
        return {"z": lax.rem(z + d, 4)}

    def near_peer(d):
        q = lax.rem(near + d, 8)
        return {"u": q // 4, "v": lax.rem(q // 2, 2), "k": lax.rem(q, 2)}

    def plane_peer(d):
        q = lax.rem(plane + d, 16)
        return {"x": q // 4, "z": lax.rem(q, 4)}

    barrier = pltpu.get_barrier_semaphore()
    for d in range(1, 8):
        for peer in (row_peer(d)[1], col_peer(d)[1]):
            pl.semaphore_signal(barrier, inc=1, device_id=peer, device_id_type=MESH)
    pl.semaphore_signal(barrier, inc=1, device_id={"k": other}, device_id_type=MESH)

    local = []
    for i, (src, dst) in enumerate((
        (ti, tiv), (qi, qiv), (tg, tgv), (qg, qgv), (bo_hbm, bo), (bi_hbm, bi), (eig_hbm, eig)
    )):
        local.append(pltpu.make_async_copy(src, dst, lsem.at[i]))
        local[-1].start()
    for copy in local[:4]:
        copy.wait()
    for rows, train, query in ((xi, tiv, qiv), (gi, tgv, qgv)):
        rows[...] = jnp.concatenate(
            [train[...].astype(F32), query[...].astype(F32), jnp.zeros((2, D_IN), F32)], axis=0
        ).astype(BF)
    pl.semaphore_wait(barrier, 15)

    for d in range(1, 8):
        q, peer = row_peer(d)
        send(
            xi.at[:, pl.ds(pl.multiple_of(q * 1024, 1024), 1024)], ra.at[r],
            ssem.at[1], rsem.at[1], peer,
        )
        q, peer = col_peer(d)
        send(
            gi.at[:, pl.ds(pl.multiple_of(q * 1024, 1024), 1024)], rb.at[2 * z + v],
            ssem.at[2], rsem.at[2], peer,
        )
    first = (
        arrival(ra.at[0:7], ssem.at[1], rsem.at[1], row_peer(1)[1]),
        arrival(rb.at[0:7], ssem.at[2], rsem.at[2], col_peer(1)[1]),
    )
    ra[r] = xi[:, pl.ds(pl.multiple_of(r * 1024, 1024), 1024)]
    rb[2 * z + v] = gi[:, pl.ds(pl.multiple_of(p * 1024, 1024), 1024)]
    pick = one_hot(48, 64, compact_source)
    local[4].wait()
    basis_copy = send(
        bo.at[:, pl.ds(pl.multiple_of(other * 512, 512), 512)],
        bfull.at[pl.ds(pl.multiple_of(k * 512, 512), 512)],
        ssem.at[0], rsem.at[0], {"k": other},
    )
    turn[...] = one_hot(128, 128, swapped_source)
    lanes = lax.broadcasted_iota(jnp.int32, (1, 256), 1)
    true_rows[...] = 2 * device_of(lanes) + lanes % 2

    moving = {}

    def wait(*key):
        moving.pop(key).wait()

    def sems(side, c, step):
        return ssem.at[3 + side * 3 + c], rsem.at[3 + (side * 3 + c) * 7 + step]

    gathered = (ai, ag)
    gather_at = ((z, v), (x, u))
    gather_y_peer = ({"v": 1 - v}, {"u": 1 - u})
    gather_peer = (z_peer, x_peer)
    sum_at = (x, z)
    sum_name = ("x", "z")
    sum_y_peer = ({"u": 1 - u}, {"v": 1 - v})
    part = (pi, pg)
    small = (si, sg)
    got = (ri, rg)
    wide_y = (yqi, yqg)
    mine_y = (wti, wtg)
    their_y = (yti, ytg)

    def gather_y(side, rows):
        at = gather_at[side]
        for c in range(3):
            ref = gathered[side].at[c, k, at[0], at[1]]
            ref[...] = rows[16 * c : 16 * c + 16]
            moving[side, c, 0] = send(ref, ref, *sems(side, c, 0), gather_y_peer[side])

    def gather_xz(side, c):
        wait(side, c, 0)
        ref = gathered[side].at[c, k, gather_at[side][0]]
        for d in range(1, 4):
            send(ref, ref, *sems(side, c, 1), gather_peer[side](d))
        moving[side, c, 1] = arrival(
            gathered[side].at[c, k, 0:3], *sems(side, c, 1), gather_peer[side](1)
        )

    def swap(c):
        for side in range(2):
            wait(side, c, 1)
            ref = gathered[side].at[c, k]
            moving[side, c, 2] = send(ref, ref, *sems(side, c, 2), {"k": other})

    def rotate(c):
        for side in range(2):
            wait(side, c, 2)
            if side == 0:
                blocks = [(0, 256, ai[c].reshape(256, 1024), bi)]
            else:
                blocks = [
                    (h * 128, 128, jnp.dot(
                        turn[...], ag[c, h].reshape(128, 1024), preferred_element_type=F32
                    ).astype(BF), bfull)
                    for h in range(2)
                ]
            for low, size, rows, basis in blocks:
                value = jnp.dot(rows, basis[...], preferred_element_type=F32)
                for b in range(4):
                    piece = value[:, b * 128 : (b + 1) * 128]
                    part[side][c, b, pl.ds(low, size)] = piece
                    small[side][c, b, pl.ds(low, size)] = piece.astype(BF)
            for d in range(1, 4):
                q = lax.rem(sum_at[side] + d, 4)
                send(
                    small[side].at[c, q], got[side].at[c, d - 1], *sems(side, c, 3),
                    {sum_name[side]: q},
                )
            moving[side, c, 3] = arrival(got[side].at[c], *sems(side, c, 3), {sum_name[side]: q})

    def reduce_y(c):
        for side in range(2):
            wait(side, c, 3)
            at = sum_at[side]
            value = part[side][c, at]
            for d in range(3):
                value = value + got[side][c, d].astype(F32)
            part[side][c, at] = value
            if c == 0:
                src, dst = part[side].at[c, at], wide_y[side]
            else:
                mine_y[side][c - 1] = value.astype(BF)
                src, dst = mine_y[side].at[c - 1], their_y[side].at[c - 1]
            moving[side, c, 4] = send(src, dst, *sems(side, c, 4), sum_y_peer[side])

    def spread(c):
        for side in range(2):
            wait(side, c, 4)
            at = sum_at[side]
            more = wide_y[side][...] if c == 0 else their_y[side][c - 1].astype(F32)
            ref = hi.at[c, at] if side == 0 else hg.at[c, k, at]
            ref[...] = (part[side][c, at] + more).astype(BF)
            peer = x_peer if side == 0 else z_peer
            for d in range(1, 4):
                send(ref, ref, *sems(side, c, 5), peer(d))
            three = hi.at[c, 0:3] if side == 0 else hg.at[c, k, 0:3]
            moving[side, c, 5] = arrival(three, *sems(side, c, 5), peer(1))

    def spread_core(c):
        wait(1, c, 5)
        moving[1, c, 6] = send(hg.at[c, k], hg.at[c, k], *sems(1, c, 6), {"k": other})

    def lay_query():
        wait(0, 0, 5)
        for b in range(4):
            a_query[pl.ds(b * 128, 128), :] = turned(hi[0, b])

    def scale(half, low, high):
        if low == 0:
            if half == 1:
                wait(1, 0, 6)
            for b in range(4):
                g_query[:, pl.ds(half * 512 + b * 128, 128)] = hg[0, (k, other)[half], b]

        def body(q, carry):
            inside = (true_rows[...] >= starts[q]) & (true_rows[...] < ends[q])
            rows = jnp.where(inside, a_query[...], 0.0).astype(BF)
            for o in range(2):
                at = pl.ds(half * 512 + o * 256, 256)
                outer = jnp.dot(rows, g_query[:, at], preferred_element_type=F32)
                scaled[q, :, at] = (outer * inverse[:, at]).astype(BF)
            return carry

        lax.fori_loop(low, high, body, 0, unroll=high - low)

    def lay_train(c):
        wait(0, c, 5)
        for b in range(4):
            a_train[c - 1, pl.ds(b * 128, 128), :] = turned(hi[c, b])
        wait(1, c, 6)
        for b in range(4):
            for s in range(2):
                block = hg[c, (k, other)[s], b]
                g_train[c - 1, pl.ds(s * 512 + b * 128, 128), :] = turned(block).astype(BF)

    def pair(c, low, high):
        def body(q, carry):
            paired = jnp.dot(scaled[q], g_train[c - 1], preferred_element_type=F32)
            acc[c - 1, pl.ds(q, 1), :] = jnp.sum(paired * a_train[c - 1], axis=0, keepdims=True)
            return carry

        lax.fori_loop(low, high, body, 0, unroll=high - low)

    def share_near(half):
        ref = near_sums.at[half, near]
        ref[...] = acc[half]
        pair_of = (ssem.at[9 + half], rsem.at[45 + half])
        for d in range(1, 8):
            send(ref, ref, *pair_of, near_peer(d))
        moving[half, 0] = arrival(near_sums.at[half, 0:7], *pair_of, near_peer(1))

    def share_plane(half):
        wait(half, 0)
        ref = plane_sums.at[half, plane]
        ref[...] = tree([near_sums[half, i] for i in range(8)])
        pair_of = (ssem.at[9 + half], rsem.at[47 + half])
        for d in range(1, 16):
            send(ref, ref, *pair_of, plane_peer(d))
        moving[half, 1] = arrival(plane_sums.at[half, 0:15], *pair_of, plane_peer(1))

    def summed(half):
        wait(half, 1)
        return tree([plane_sums[half, i] for i in range(16)])

    def in_order(value, half):
        total = 0.0
        for _ in range(3):
            piece = value.astype(BF)
            value = value - piece.astype(F32)
            total = total + jnp.dot(piece, place[half], preferred_element_type=F32)
        return total

    for side, rows in ((0, ra), (1, rb)):
        first[side].wait()
        gather_y(side, jnp.dot(pick, rows[...].reshape(64, 1024), preferred_element_type=F32).astype(BF))
    bfull[pl.ds(pl.multiple_of(k * 512, 512), 512), :] = bo[:, pl.ds(pl.multiple_of(k * 512, 512), 512)]
    for c in range(3):
        for side in range(2):
            gather_xz(side, c)

    train = lax.broadcasted_iota(jnp.int32, (1, 512), 1)
    device = train // 4
    spot = train // 2 % 2 * 256 + device % 2 * 128 + device // 2 % 4 * 32 + device % 16 // 8 * 16
    spot = spot + device // 16 * 2 + train % 2
    row = lax.broadcasted_iota(jnp.int32, (512, 512), 0)
    place[...] = jnp.where(row == spot, 1.0, 0.0).astype(BF).reshape(2, 256, 512)
    local[5].wait()
    basis_copy.wait()
    swap(0)
    rotate(0)
    swap(1)
    swap(2)
    rotate(1)
    reduce_y(0)
    rotate(2)
    local[6].wait()
    for half, at in enumerate((k, other)):
        rows = eig[pl.ds(pl.multiple_of(at * 512, 512), 512), :]
        inverse[:, pl.ds(half * 512, 512)] = jnp.transpose(1.0 / (rows + damping), (1, 0))
    spread(0)
    reduce_y(1)
    reduce_y(2)
    spread(1)
    spread_core(0)
    lay_query()
    scale(0, 0, 16)
    spread(2)
    scale(1, 0, 8)
    spread_core(1)
    scale(1, 8, 16)
    spread_core(2)
    lay_train(1)
    pair(1, 0, 16)
    share_near(0)
    lay_train(2)
    pair(2, 0, 16)
    share_near(1)
    share_plane(0)
    share_plane(1)
    early = in_order(summed(0), 0)
    total = early + in_order(summed(1), 1)
    out[...] = total * (1.0 / math.sqrt(D_IN * D_OUT * QBLOCK))


def shards(
    train_inputs,
    train_grads,
    query_inputs,
    query_grads,
    input_basis,
    output_basis,
    eigenvalues,
    query_starts,
    query_ends,
):
    vmem = pl.BlockSpec(memory_space=pltpu.VMEM)
    smem = pl.BlockSpec(memory_space=pltpu.SMEM)
    return pl.pallas_call(
        kernel,
        out_shape=jax.ShapeDtypeStruct((NQ, 512), F32),
        in_specs=[smem, smem] + [pl.BlockSpec(memory_space=pl.ANY)] * 7,
        out_specs=vmem,
        scratch_shapes=[
            pltpu.VMEM((4, 8192), BF),
            pltpu.VMEM((2, 8192), BF),
            pltpu.VMEM((4, 8192), BF),
            pltpu.VMEM((2, 8192), BF),
            pltpu.VMEM((1024, 512), BF),
            pltpu.VMEM((512, 1024), BF),
            pltpu.VMEM((1024, 512), F32),
            pltpu.VMEM((8, 8192), BF),
            pltpu.VMEM((8, 8192), BF),
            pltpu.VMEM((8, 8, 1024), BF),
            pltpu.VMEM((8, 8, 1024), BF),
            pltpu.VMEM((3, 2, 4, 2, 16, 1024), BF),
            pltpu.VMEM((3, 2, 4, 2, 16, 1024), BF),
            pltpu.VMEM((1024, 512), BF),
            pltpu.VMEM((3, 4, 256, 128), F32),
            pltpu.VMEM((3, 4, 256, 128), F32),
            pltpu.VMEM((3, 4, 256, 128), BF),
            pltpu.VMEM((3, 4, 256, 128), BF),
            pltpu.VMEM((3, 3, 256, 128), BF),
            pltpu.VMEM((3, 3, 256, 128), BF),
            pltpu.VMEM((256, 128), F32),
            pltpu.VMEM((256, 128), F32),
            pltpu.VMEM((2, 256, 128), BF),
            pltpu.VMEM((2, 256, 128), BF),
            pltpu.VMEM((2, 256, 128), BF),
            pltpu.VMEM((2, 256, 128), BF),
            pltpu.VMEM((3, 4, 256, 128), BF),
            pltpu.VMEM((3, 2, 4, 256, 128), BF),
            pltpu.VMEM((512, 1024), F32),
            pltpu.VMEM((512, 256), F32),
            pltpu.VMEM((256, 1024), BF),
            pltpu.VMEM((2, 512, 256), F32),
            pltpu.VMEM((2, 1024, 256), BF),
            pltpu.VMEM((NQ, 512, 1024), BF),
            pltpu.VMEM((2, NQ, 256), F32),
            pltpu.VMEM((128, 128), BF),
            pltpu.VMEM((2, 256, 512), BF),
            pltpu.VMEM((1, 256), jnp.int32),
            pltpu.VMEM((2, 8, NQ, 256), F32),
            pltpu.VMEM((2, 16, NQ, 256), F32),
            pltpu.SemaphoreType.DMA((7,)),
            pltpu.SemaphoreType.DMA((11,)),
            pltpu.SemaphoreType.DMA((49,)),
        ],
        compiler_params=pltpu.CompilerParams(
            collective_id=0, has_side_effects=True, vmem_limit_bytes=56 * 2**20
        ),
    )(
        query_starts, query_ends, train_inputs, query_inputs, train_grads, query_grads,
        input_basis, output_basis, eigenvalues,
    )


def solution(mesh):
    split = Mesh(mesh.devices.reshape(4, 2, 2, 4, 2), ALL)
    placed = (
        P(ROW + COL, None),
        P(ROW + COL, None),
        P(ROW + COL, None),
        P(ROW + COL, None),
        P(ROW, COL),
        P(COL, ROW),
        P(ROW, COL),
        P(),
        P(),
    )
    return jax.shard_map(shards, mesh=split, in_specs=placed, out_specs=P(), check_vma=False)
```

```python
import math

import jax
import jax.numpy as jnp
from jax import lax
from jax.experimental import pallas as pl
from jax.experimental.pallas import tpu as pltpu
from jax.sharding import Mesh
from jax.sharding import PartitionSpec as P

D_IN = 8192
D_OUT = 8192
QBLOCK = 128
NQ = 16
MESH = pl.DeviceIdType.MESH
ROW = ("x", "u")
COL = ("v", "z", "k")
ALL = ("x", "u", "v", "z", "k")
damping = 0.1
BF = jnp.bfloat16
F32 = jnp.float32


def send(src, dst, send_sem, recv_sem, device):
    copy = pltpu.make_async_remote_copy(
        src_ref=src,
        dst_ref=dst,
        send_sem=send_sem,
        recv_sem=recv_sem,
        device_id=device,
        device_id_type=MESH,
    )
    copy.start()
    return copy


def arrival(ref, send_sem, recv_sem, device):
    return pltpu.make_async_remote_copy(
        src_ref=ref,
        dst_ref=ref,
        send_sem=send_sem,
        recv_sem=recv_sem,
        device_id=device,
        device_id_type=MESH,
    )


def one_hot(rows, cols, source):
    row = lax.broadcasted_iota(jnp.int32, (rows, 1), 0)
    col = lax.broadcasted_iota(jnp.int32, (rows, cols), 1)
    return jnp.where(col == source(row), 1.0, 0.0).astype(BF)


def compact_source(row):
    chunk, inner = row // 16, row % 16
    first = jnp.where(chunk == 0, 4, 2 * chunk - 2)
    return inner // 2 * 8 + first + inner % 2


def swapped_source(row):
    outer, inner, j = row // 16, row // 2 % 8, row % 2
    return inner * 16 + outer * 2 + j


def device_of(row):
    k, z, v = row // 128, row // 32 % 4, row // 16 % 2
    x, u = row // 4 % 4, row // 2 % 2
    return 16 * (2 * x + u) + 8 * v + 2 * z + k


def tree(values):
    while len(values) > 1:
        values = [a + b for a, b in zip(values[::2], values[1::2])]
    return values[0]


def turned(block):
    return jnp.transpose(block.astype(F32), (1, 0))


def kernel(
    starts, ends, ti, qi, tg, qg, bi_hbm, bo_hbm, eig_hbm, out,
    tiv, qiv, tgv, qgv, bi, bo, eig,
    xi, gi, ra, rb, ai, ag, bfull, pi, pg, si, sg, ri, rg, yqi, yqg, yti, ytg, wti, wtg, hi, hg,
    inverse, a_query, g_query, a_train, g_train, scaled, acc, turn, place, true_rows, near_sums, plane_sums,
    lsem, ssem, rsem,
):
    x, u, v, z, k = (lax.axis_index(a) for a in ALL)
    r, p = x * 2 + u, v * 4 + z
    other = 1 - k
    near, plane = u * 4 + v * 2 + k, x * 4 + z

    def row_peer(d):
        q = lax.rem(r + d, 8)
        return q, {"x": q // 2, "u": lax.rem(q, 2)}

    def col_peer(d):
        q = lax.rem(p + d, 8)
        return q, {"v": q // 4, "z": lax.rem(q, 4)}

    def x_peer(d):
        return {"x": lax.rem(x + d, 4)}

    def z_peer(d):
        return {"z": lax.rem(z + d, 4)}

    def near_peer(d):
        q = lax.rem(near + d, 8)
        return {"u": q // 4, "v": lax.rem(q // 2, 2), "k": lax.rem(q, 2)}

    def plane_peer(d):
        q = lax.rem(plane + d, 16)
        return {"x": q // 4, "z": lax.rem(q, 4)}

    barrier = pltpu.get_barrier_semaphore()
    for d in range(1, 8):
        for peer in (row_peer(d)[1], col_peer(d)[1]):
            pl.semaphore_signal(barrier, inc=1, device_id=peer, device_id_type=MESH)
    pl.semaphore_signal(barrier, inc=1, device_id={"k": other}, device_id_type=MESH)

    local = []
    for i, (src, dst) in enumerate((
        (ti, tiv), (qi, qiv), (tg, tgv), (qg, qgv), (bo_hbm, bo), (bi_hbm, bi), (eig_hbm, eig)
    )):
        local.append(pltpu.make_async_copy(src, dst, lsem.at[i]))
        local[-1].start()
    for copy in local[:4]:
        copy.wait()
    for rows, train, query in ((xi, tiv, qiv), (gi, tgv, qgv)):
        rows[...] = jnp.concatenate(
            [train[...].astype(F32), query[...].astype(F32), jnp.zeros((2, D_IN), F32)], axis=0
        ).astype(BF)
    pl.semaphore_wait(barrier, 15)

    for d in range(1, 8):
        q, peer = row_peer(d)
        send(
            xi.at[:, pl.ds(pl.multiple_of(q * 1024, 1024), 1024)], ra.at[r],
            ssem.at[1], rsem.at[1], peer,
        )
        q, peer = col_peer(d)
        send(
            gi.at[:, pl.ds(pl.multiple_of(q * 1024, 1024), 1024)], rb.at[2 * z + v],
            ssem.at[2], rsem.at[2], peer,
        )
    first = (
        arrival(ra.at[0:7], ssem.at[1], rsem.at[1], row_peer(1)[1]),
        arrival(rb.at[0:7], ssem.at[2], rsem.at[2], col_peer(1)[1]),
    )
    ra[r] = xi[:, pl.ds(pl.multiple_of(r * 1024, 1024), 1024)]
    rb[2 * z + v] = gi[:, pl.ds(pl.multiple_of(p * 1024, 1024), 1024)]
    pick = one_hot(48, 64, compact_source)
    local[4].wait()
    basis_copy = send(
        bo.at[:, pl.ds(pl.multiple_of(other * 512, 512), 512)],
        bfull.at[pl.ds(pl.multiple_of(k * 512, 512), 512)],
        ssem.at[0], rsem.at[0], {"k": other},
    )
    turn[...] = one_hot(128, 128, swapped_source)
    lanes = lax.broadcasted_iota(jnp.int32, (1, 256), 1)
    true_rows[...] = 2 * device_of(lanes) + lanes % 2

    moving = {}

    def wait(*key):
        moving.pop(key).wait()

    def sems(side, c, step):
        return ssem.at[3 + side * 3 + c], rsem.at[3 + (side * 3 + c) * 7 + step]

    gathered = (ai, ag)
    gather_at = ((z, v), (x, u))
    gather_y_peer = ({"v": 1 - v}, {"u": 1 - u})
    gather_peer = (z_peer, x_peer)
    sum_at = (x, z)
    sum_name = ("x", "z")
    sum_y_peer = ({"u": 1 - u}, {"v": 1 - v})
    part = (pi, pg)
    small = (si, sg)
    got = (ri, rg)
    wide_y = (yqi, yqg)
    mine_y = (wti, wtg)
    their_y = (yti, ytg)

    def gather_y(side, rows):
        at = gather_at[side]
        for c in range(3):
            ref = gathered[side].at[c, k, at[0], at[1]]
            ref[...] = rows[16 * c : 16 * c + 16]
            moving[side, c, 0] = send(ref, ref, *sems(side, c, 0), gather_y_peer[side])

    def gather_xz(side, c):
        wait(side, c, 0)
        ref = gathered[side].at[c, k, gather_at[side][0]]
        for d in range(1, 4):
            send(ref, ref, *sems(side, c, 1), gather_peer[side](d))
        moving[side, c, 1] = arrival(
            gathered[side].at[c, k, 0:3], *sems(side, c, 1), gather_peer[side](1)
        )

    def swap(c):
        for side in range(2):
            wait(side, c, 1)
            ref = gathered[side].at[c, k]
            moving[side, c, 2] = send(ref, ref, *sems(side, c, 2), {"k": other})

    def rotate(c):
        for side in range(2):
            wait(side, c, 2)
            if side == 0:
                blocks = [(0, 256, ai[c].reshape(256, 1024), bi)]
            else:
                blocks = [
                    (h * 128, 128, jnp.dot(
                        turn[...], ag[c, h].reshape(128, 1024), preferred_element_type=F32
                    ).astype(BF), bfull)
                    for h in range(2)
                ]
            for low, size, rows, basis in blocks:
                value = jnp.dot(rows, basis[...], preferred_element_type=F32)
                for b in range(4):
                    piece = value[:, b * 128 : (b + 1) * 128]
                    part[side][c, b, pl.ds(low, size)] = piece
                    small[side][c, b, pl.ds(low, size)] = piece.astype(BF)
            for d in range(1, 4):
                q = lax.rem(sum_at[side] + d, 4)
                send(
                    small[side].at[c, q], got[side].at[c, d - 1], *sems(side, c, 3),
                    {sum_name[side]: q},
                )
            moving[side, c, 3] = arrival(got[side].at[c], *sems(side, c, 3), {sum_name[side]: q})

    def reduce_y(c):
        for side in range(2):
            wait(side, c, 3)
            at = sum_at[side]
            value = part[side][c, at]
            for d in range(3):
                value = value + got[side][c, d].astype(F32)
            part[side][c, at] = value
            if c == 0:
                src, dst = part[side].at[c, at], wide_y[side]
            else:
                mine_y[side][c - 1] = value.astype(BF)
                src, dst = mine_y[side].at[c - 1], their_y[side].at[c - 1]
            moving[side, c, 4] = send(src, dst, *sems(side, c, 4), sum_y_peer[side])

    def spread(c):
        for side in range(2):
            wait(side, c, 4)
            at = sum_at[side]
            more = wide_y[side][...] if c == 0 else their_y[side][c - 1].astype(F32)
            ref = hi.at[c, at] if side == 0 else hg.at[c, k, at]
            ref[...] = (part[side][c, at] + more).astype(BF)
            peer = x_peer if side == 0 else z_peer
            for d in range(1, 4):
                send(ref, ref, *sems(side, c, 5), peer(d))
            three = hi.at[c, 0:3] if side == 0 else hg.at[c, k, 0:3]
            moving[side, c, 5] = arrival(three, *sems(side, c, 5), peer(1))

    def spread_core(c):
        wait(1, c, 5)
        moving[1, c, 6] = send(hg.at[c, k], hg.at[c, k], *sems(1, c, 6), {"k": other})

    def lay_query():
        wait(0, 0, 5)
        for b in range(4):
            a_query[pl.ds(b * 128, 128), :] = turned(hi[0, b])

    def scale(half, low, high):
        if low == 0:
            if half == 1:
                wait(1, 0, 6)
            for b in range(4):
                g_query[:, pl.ds(half * 512 + b * 128, 128)] = hg[0, (k, other)[half], b]

        def body(q, carry):
            inside = (true_rows[...] >= starts[q]) & (true_rows[...] < ends[q])
            rows = jnp.where(inside, a_query[...], 0.0).astype(BF)
            for o in range(2):
                at = pl.ds(half * 512 + o * 256, 256)
                outer = jnp.dot(rows, g_query[:, at], preferred_element_type=F32)
                scaled[q, :, at] = (outer * inverse[:, at]).astype(BF)
            return carry

        lax.fori_loop(low, high, body, 0, unroll=high - low)

    def lay_train(c):
        wait(0, c, 5)
        for b in range(4):
            a_train[c - 1, pl.ds(b * 128, 128), :] = turned(hi[c, b])
        wait(1, c, 6)
        for b in range(4):
            for s in range(2):
                block = hg[c, (k, other)[s], b]
                g_train[c - 1, pl.ds(s * 512 + b * 128, 128), :] = turned(block).astype(BF)

    def pair(c, low, high):
        def body(q, carry):
            paired = jnp.dot(scaled[q], g_train[c - 1], preferred_element_type=F32)
            acc[c - 1, pl.ds(q, 1), :] = jnp.sum(paired * a_train[c - 1], axis=0, keepdims=True)
            return carry

        lax.fori_loop(low, high, body, 0, unroll=high - low)

    pieces = ((0, 0, 16), (1, 0, 8), (1, 8, 8))

    def share_near(i):
        half, low, size = pieces[i]
        rows = pl.ds(0, size)
        near_sums[i, near, rows, :] = acc[half, pl.ds(low, size), :]
        ref = near_sums.at[i, near, rows]
        pair_of = (ssem.at[9 + i], rsem.at[45 + i])
        for d in range(1, 8):
            send(ref, ref, *pair_of, near_peer(d))
        moving["near", i] = arrival(near_sums.at[i, 0:7, rows], *pair_of, near_peer(1))

    def share_plane(i):
        wait("near", i)
        rows = pl.ds(0, pieces[i][2])
        plane_sums[i, plane, rows, :] = tree([near_sums[i, j, rows, :] for j in range(8)])
        ref = plane_sums.at[i, plane, rows]
        pair_of = (ssem.at[9 + i], rsem.at[48 + i])
        for d in range(1, 16):
            send(ref, ref, *pair_of, plane_peer(d))
        moving["plane", i] = arrival(plane_sums.at[i, 0:15, rows], *pair_of, plane_peer(1))

    def summed(i):
        wait("plane", i)
        rows = pl.ds(0, pieces[i][2])
        return tree([plane_sums[i, j, rows, :] for j in range(16)])

    def in_order(value, half):
        total = 0.0
        for _ in range(3):
            piece = value.astype(BF)
            value = value - piece.astype(F32)
            total = total + jnp.dot(piece, place[half], preferred_element_type=F32)
        return total

    for side, rows in ((0, ra), (1, rb)):
        first[side].wait()
        gather_y(side, jnp.dot(pick, rows[...].reshape(64, 1024), preferred_element_type=F32).astype(BF))
    bfull[pl.ds(pl.multiple_of(k * 512, 512), 512), :] = bo[:, pl.ds(pl.multiple_of(k * 512, 512), 512)]
    for c in range(3):
        for side in range(2):
            gather_xz(side, c)

    train = lax.broadcasted_iota(jnp.int32, (1, 512), 1)
    device = train // 4
    spot = train // 2 % 2 * 256 + device % 2 * 128 + device // 2 % 4 * 32 + device % 16 // 8 * 16
    spot = spot + device // 16 * 2 + train % 2
    row = lax.broadcasted_iota(jnp.int32, (512, 512), 0)
    place[...] = jnp.where(row == spot, 1.0, 0.0).astype(BF).reshape(2, 256, 512)
    local[5].wait()
    basis_copy.wait()
    swap(0)
    rotate(0)
    swap(1)
    swap(2)
    rotate(1)
    reduce_y(0)
    rotate(2)
    local[6].wait()
    for half, at in enumerate((k, other)):
        rows = eig[pl.ds(pl.multiple_of(at * 512, 512), 512), :]
        inverse[:, pl.ds(half * 512, 512)] = jnp.transpose(1.0 / (rows + damping), (1, 0))
    spread(0)
    reduce_y(1)
    reduce_y(2)
    spread_core(0)
    lay_query()
    spread(1)
    scale(0, 0, 8)
    spread(2)
    scale(0, 8, 16)
    scale(1, 0, 16)
    spread_core(1)
    lay_train(1)
    pair(1, 0, 8)
    spread_core(2)
    pair(1, 8, 16)
    share_near(0)
    lay_train(2)
    pair(2, 0, 8)
    share_near(1)
    pair(2, 8, 16)
    share_near(2)
    share_plane(0)
    share_plane(1)
    early = in_order(summed(0), 0)
    share_plane(2)
    late = in_order(jnp.concatenate([summed(1), summed(2)], axis=0), 1)
    total = early + late
    out[...] = total * (1.0 / math.sqrt(D_IN * D_OUT * QBLOCK))


def shards(
    train_inputs,
    train_grads,
    query_inputs,
    query_grads,
    input_basis,
    output_basis,
    eigenvalues,
    query_starts,
    query_ends,
):
    vmem = pl.BlockSpec(memory_space=pltpu.VMEM)
    smem = pl.BlockSpec(memory_space=pltpu.SMEM)
    return pl.pallas_call(
        kernel,
        out_shape=jax.ShapeDtypeStruct((NQ, 512), F32),
        in_specs=[smem, smem] + [pl.BlockSpec(memory_space=pl.ANY)] * 7,
        out_specs=vmem,
        scratch_shapes=[
            pltpu.VMEM((4, 8192), BF),
            pltpu.VMEM((2, 8192), BF),
            pltpu.VMEM((4, 8192), BF),
            pltpu.VMEM((2, 8192), BF),
            pltpu.VMEM((1024, 512), BF),
            pltpu.VMEM((512, 1024), BF),
            pltpu.VMEM((1024, 512), F32),
            pltpu.VMEM((8, 8192), BF),
            pltpu.VMEM((8, 8192), BF),
            pltpu.VMEM((8, 8, 1024), BF),
            pltpu.VMEM((8, 8, 1024), BF),
            pltpu.VMEM((3, 2, 4, 2, 16, 1024), BF),
            pltpu.VMEM((3, 2, 4, 2, 16, 1024), BF),
            pltpu.VMEM((1024, 512), BF),
            pltpu.VMEM((3, 4, 256, 128), F32),
            pltpu.VMEM((3, 4, 256, 128), F32),
            pltpu.VMEM((3, 4, 256, 128), BF),
            pltpu.VMEM((3, 4, 256, 128), BF),
            pltpu.VMEM((3, 3, 256, 128), BF),
            pltpu.VMEM((3, 3, 256, 128), BF),
            pltpu.VMEM((256, 128), F32),
            pltpu.VMEM((256, 128), F32),
            pltpu.VMEM((2, 256, 128), BF),
            pltpu.VMEM((2, 256, 128), BF),
            pltpu.VMEM((2, 256, 128), BF),
            pltpu.VMEM((2, 256, 128), BF),
            pltpu.VMEM((3, 4, 256, 128), BF),
            pltpu.VMEM((3, 2, 4, 256, 128), BF),
            pltpu.VMEM((512, 1024), F32),
            pltpu.VMEM((512, 256), F32),
            pltpu.VMEM((256, 1024), BF),
            pltpu.VMEM((2, 512, 256), F32),
            pltpu.VMEM((2, 1024, 256), BF),
            pltpu.VMEM((NQ, 512, 1024), BF),
            pltpu.VMEM((2, NQ, 256), F32),
            pltpu.VMEM((128, 128), BF),
            pltpu.VMEM((2, 256, 512), BF),
            pltpu.VMEM((1, 256), jnp.int32),
            pltpu.VMEM((3, 8, NQ, 256), F32),
            pltpu.VMEM((3, 16, NQ, 256), F32),
            pltpu.SemaphoreType.DMA((7,)),
            pltpu.SemaphoreType.DMA((12,)),
            pltpu.SemaphoreType.DMA((51,)),
        ],
        compiler_params=pltpu.CompilerParams(
            collective_id=0, has_side_effects=True, vmem_limit_bytes=56 * 2**20
        ),
    )(
        query_starts, query_ends, train_inputs, query_inputs, train_grads, query_grads,
        input_basis, output_basis, eigenvalues,
    )


def solution(mesh):
    split = Mesh(mesh.devices.reshape(4, 2, 2, 4, 2), ALL)
    placed = (
        P(ROW + COL, None),
        P(ROW + COL, None),
        P(ROW + COL, None),
        P(ROW + COL, None),
        P(ROW, COL),
        P(COL, ROW),
        P(ROW, COL),
        P(),
        P(),
    )
    return jax.shard_map(shards, mesh=split, in_specs=placed, out_specs=P(), check_vma=False)
```

```python
import math

import jax
import jax.numpy as jnp
from jax import lax
from jax.experimental import pallas as pl
from jax.experimental.pallas import tpu as pltpu
from jax.sharding import Mesh
from jax.sharding import PartitionSpec as P

D_IN = 8192
D_OUT = 8192
QBLOCK = 128
NQ = 16
MESH = pl.DeviceIdType.MESH
ROW = ("x", "u")
COL = ("v", "z", "k")
ALL = ("x", "u", "v", "z", "k")
damping = 0.1
BF = jnp.bfloat16
F32 = jnp.float32


def send(src, dst, send_sem, recv_sem, device):
    copy = pltpu.make_async_remote_copy(
        src_ref=src,
        dst_ref=dst,
        send_sem=send_sem,
        recv_sem=recv_sem,
        device_id=device,
        device_id_type=MESH,
    )
    copy.start()
    return copy


def arrival(ref, send_sem, recv_sem, device):
    return pltpu.make_async_remote_copy(
        src_ref=ref,
        dst_ref=ref,
        send_sem=send_sem,
        recv_sem=recv_sem,
        device_id=device,
        device_id_type=MESH,
    )


def one_hot(rows, cols, source):
    row = lax.broadcasted_iota(jnp.int32, (rows, 1), 0)
    col = lax.broadcasted_iota(jnp.int32, (rows, cols), 1)
    return jnp.where(col == source(row), 1.0, 0.0).astype(BF)


def compact_source(row):
    chunk, inner = row // 16, row % 16
    first = jnp.where(chunk == 0, 4, 2 * chunk - 2)
    return inner // 2 * 8 + first + inner % 2


def swapped_source(row):
    outer, inner, j = row // 16, row // 2 % 8, row % 2
    return inner * 16 + outer * 2 + j


def device_of(row):
    k, z, v = row // 128, row // 32 % 4, row // 16 % 2
    x, u = row // 4 % 4, row // 2 % 2
    return 16 * (2 * x + u) + 8 * v + 2 * z + k


def tree(values):
    while len(values) > 1:
        values = [a + b for a, b in zip(values[::2], values[1::2])]
    return values[0]


def turned(block):
    return jnp.transpose(block.astype(F32), (1, 0))


def kernel(
    starts, ends, ti, qi, tg, qg, bi_hbm, bo_hbm, eig_hbm, out,
    tiv, qiv, tgv, qgv, bi, bo, eig,
    xi, gi, ra, rb, ai, ag, bfull, pi, pg, si, sg, ri, rg, yqi, yqg, yti, ytg, wti, wtg, hi, hg,
    inverse, a_query, g_query, a_train, g_train, scaled, acc, turn, place, true_rows, near_sums, plane_sums,
    lsem, ssem, rsem,
):
    x, u, v, z, k = (lax.axis_index(a) for a in ALL)
    r, p = x * 2 + u, v * 4 + z
    other = 1 - k
    near, plane = u * 4 + v * 2 + k, x * 4 + z

    def row_peer(d):
        q = lax.rem(r + d, 8)
        return q, {"x": q // 2, "u": lax.rem(q, 2)}

    def col_peer(d):
        q = lax.rem(p + d, 8)
        return q, {"v": q // 4, "z": lax.rem(q, 4)}

    def x_peer(d):
        return {"x": lax.rem(x + d, 4)}

    def z_peer(d):
        return {"z": lax.rem(z + d, 4)}

    def near_peer(d):
        q = lax.rem(near + d, 8)
        return {"u": q // 4, "v": lax.rem(q // 2, 2), "k": lax.rem(q, 2)}

    def plane_peer(d):
        q = lax.rem(plane + d, 16)
        return {"x": q // 4, "z": lax.rem(q, 4)}

    barrier = pltpu.get_barrier_semaphore()
    for d in range(1, 8):
        for peer in (row_peer(d)[1], col_peer(d)[1]):
            pl.semaphore_signal(barrier, inc=1, device_id=peer, device_id_type=MESH)
    pl.semaphore_signal(barrier, inc=1, device_id={"k": other}, device_id_type=MESH)

    local = []
    for i, (src, dst) in enumerate((
        (ti, tiv), (qi, qiv), (tg, tgv), (qg, qgv), (bo_hbm, bo), (bi_hbm, bi), (eig_hbm, eig)
    )):
        local.append(pltpu.make_async_copy(src, dst, lsem.at[i]))
        local[-1].start()
    for copy in local[:4]:
        copy.wait()
    for rows, train, query in ((xi, tiv, qiv), (gi, tgv, qgv)):
        rows[...] = jnp.concatenate(
            [train[...].astype(F32), query[...].astype(F32), jnp.zeros((2, D_IN), F32)], axis=0
        ).astype(BF)
    pl.semaphore_wait(barrier, 15)

    for d in range(1, 8):
        q, peer = row_peer(d)
        send(
            xi.at[:, pl.ds(pl.multiple_of(q * 1024, 1024), 1024)], ra.at[r],
            ssem.at[1], rsem.at[1], peer,
        )
        q, peer = col_peer(d)
        send(
            gi.at[:, pl.ds(pl.multiple_of(q * 1024, 1024), 1024)], rb.at[2 * z + v],
            ssem.at[2], rsem.at[2], peer,
        )
    first = (
        arrival(ra.at[0:7], ssem.at[1], rsem.at[1], row_peer(1)[1]),
        arrival(rb.at[0:7], ssem.at[2], rsem.at[2], col_peer(1)[1]),
    )
    ra[r] = xi[:, pl.ds(pl.multiple_of(r * 1024, 1024), 1024)]
    rb[2 * z + v] = gi[:, pl.ds(pl.multiple_of(p * 1024, 1024), 1024)]
    pick = one_hot(48, 64, compact_source)
    local[4].wait()
    basis_copy = send(
        bo.at[:, pl.ds(pl.multiple_of(other * 512, 512), 512)],
        bfull.at[pl.ds(pl.multiple_of(k * 512, 512), 512)],
        ssem.at[0], rsem.at[0], {"k": other},
    )
    turn[...] = one_hot(128, 128, swapped_source)
    lanes = lax.broadcasted_iota(jnp.int32, (1, 256), 1)
    true_rows[...] = 2 * device_of(lanes) + lanes % 2

    moving = {}

    def wait(*key):
        moving.pop(key).wait()

    def sems(side, c, step):
        return ssem.at[3 + side * 3 + c], rsem.at[3 + (side * 3 + c) * 7 + step]

    gathered = (ai, ag)
    gather_at = ((z, v), (x, u))
    gather_y_peer = ({"v": 1 - v}, {"u": 1 - u})
    gather_peer = (z_peer, x_peer)
    sum_at = (x, z)
    sum_name = ("x", "z")
    sum_y_peer = ({"u": 1 - u}, {"v": 1 - v})
    part = (pi, pg)
    small = (si, sg)
    got = (ri, rg)
    wide_y = (yqi, yqg)
    mine_y = (wti, wtg)
    their_y = (yti, ytg)

    def gather_y(side, rows):
        at = gather_at[side]
        for c in range(3):
            ref = gathered[side].at[c, k, at[0], at[1]]
            ref[...] = rows[16 * c : 16 * c + 16]
            moving[side, c, 0] = send(ref, ref, *sems(side, c, 0), gather_y_peer[side])

    def gather_xz(side, c):
        wait(side, c, 0)
        ref = gathered[side].at[c, k, gather_at[side][0]]
        for d in (2, 1, 3):
            send(ref, ref, *sems(side, c, 1), gather_peer[side](d))
        moving[side, c, 1] = arrival(
            gathered[side].at[c, k, 0:3], *sems(side, c, 1), gather_peer[side](1)
        )

    def swap(c):
        for side in range(2):
            wait(side, c, 1)
            ref = gathered[side].at[c, k]
            moving[side, c, 2] = send(ref, ref, *sems(side, c, 2), {"k": other})

    def rotate(c):
        for side in range(2):
            wait(side, c, 2)
            if side == 0:
                blocks = [(0, 256, ai[c].reshape(256, 1024), bi)]
            else:
                blocks = [
                    (h * 128, 128, jnp.dot(
                        turn[...], ag[c, h].reshape(128, 1024), preferred_element_type=F32
                    ).astype(BF), bfull)
                    for h in range(2)
                ]
            for low, size, rows, basis in blocks:
                value = jnp.dot(rows, basis[...], preferred_element_type=F32)
                for b in range(4):
                    piece = value[:, b * 128 : (b + 1) * 128]
                    part[side][c, b, pl.ds(low, size)] = piece
                    small[side][c, b, pl.ds(low, size)] = piece.astype(BF)
            for d in (2, 1, 3):
                q = lax.rem(sum_at[side] + d, 4)
                send(
                    small[side].at[c, q], got[side].at[c, d - 1], *sems(side, c, 3),
                    {sum_name[side]: q},
                )
            moving[side, c, 3] = arrival(got[side].at[c], *sems(side, c, 3), {sum_name[side]: q})

    def reduce_y(c):
        for side in range(2):
            wait(side, c, 3)
            at = sum_at[side]
            value = part[side][c, at]
            for d in range(3):
                value = value + got[side][c, d].astype(F32)
            part[side][c, at] = value
            if c == 0:
                src, dst = part[side].at[c, at], wide_y[side]
            else:
                mine_y[side][c - 1] = value.astype(BF)
                src, dst = mine_y[side].at[c - 1], their_y[side].at[c - 1]
            moving[side, c, 4] = send(src, dst, *sems(side, c, 4), sum_y_peer[side])

    def spread(c):
        for side in range(2):
            wait(side, c, 4)
            at = sum_at[side]
            more = wide_y[side][...] if c == 0 else their_y[side][c - 1].astype(F32)
            ref = hi.at[c, at] if side == 0 else hg.at[c, k, at]
            ref[...] = (part[side][c, at] + more).astype(BF)
            peer = x_peer if side == 0 else z_peer
            for d in (2, 1, 3):
                send(ref, ref, *sems(side, c, 5), peer(d))
            three = hi.at[c, 0:3] if side == 0 else hg.at[c, k, 0:3]
            moving[side, c, 5] = arrival(three, *sems(side, c, 5), peer(1))

    def spread_core(c):
        wait(1, c, 5)
        moving[1, c, 6] = send(hg.at[c, k], hg.at[c, k], *sems(1, c, 6), {"k": other})

    def lay_query():
        wait(0, 0, 5)
        for b in range(4):
            a_query[pl.ds(b * 128, 128), :] = turned(hi[0, b])

    def scale(half, low, high):
        if low == 0:
            if half == 1:
                wait(1, 0, 6)
            for b in range(4):
                g_query[:, pl.ds(half * 512 + b * 128, 128)] = hg[0, (k, other)[half], b]

        def body(q, carry):
            inside = (true_rows[...] >= starts[q]) & (true_rows[...] < ends[q])
            rows = jnp.where(inside, a_query[...], 0.0).astype(BF)
            for o in range(2):
                at = pl.ds(half * 512 + o * 256, 256)
                outer = jnp.dot(rows, g_query[:, at], preferred_element_type=F32)
                scaled[q, :, at] = (outer * inverse[:, at]).astype(BF)
            return carry

        lax.fori_loop(low, high, body, 0, unroll=high - low)

    def lay_train(c):
        wait(0, c, 5)
        for b in range(4):
            a_train[c - 1, pl.ds(b * 128, 128), :] = turned(hi[c, b])
        wait(1, c, 6)
        for b in range(4):
            for s in range(2):
                block = hg[c, (k, other)[s], b]
                g_train[c - 1, pl.ds(s * 512 + b * 128, 128), :] = turned(block).astype(BF)

    def pair(c, low, high):
        def body(q, carry):
            paired = jnp.dot(scaled[q], g_train[c - 1], preferred_element_type=F32)
            acc[c - 1, pl.ds(q, 1), :] = jnp.sum(paired * a_train[c - 1], axis=0, keepdims=True)
            return carry

        lax.fori_loop(low, high, body, 0, unroll=high - low)

    pieces = ((0, 0, 16), (1, 0, 16))

    def share_near(i):
        half, low, size = pieces[i]
        rows = pl.ds(0, size)
        near_sums[i, near, rows, :] = acc[half, pl.ds(low, size), :]
        ref = near_sums.at[i, near, rows]
        pair_of = (ssem.at[9 + i], rsem.at[45 + i])
        for d in range(1, 8):
            send(ref, ref, *pair_of, near_peer(d))
        moving["near", i] = arrival(near_sums.at[i, 0:7, rows], *pair_of, near_peer(1))

    def share_plane(i):
        wait("near", i)
        rows = pl.ds(0, pieces[i][2])
        plane_sums[i, plane, rows, :] = tree([near_sums[i, j, rows, :] for j in range(8)])
        ref = plane_sums.at[i, plane, rows]
        pair_of = (ssem.at[9 + i], rsem.at[48 + i])
        for d in range(1, 16):
            send(ref, ref, *pair_of, plane_peer(d))
        moving["plane", i] = arrival(plane_sums.at[i, 0:15, rows], *pair_of, plane_peer(1))

    def summed(i):
        wait("plane", i)
        rows = pl.ds(0, pieces[i][2])
        return tree([plane_sums[i, j, rows, :] for j in range(16)])

    def in_order(value, half):
        total = 0.0
        for _ in range(3):
            piece = value.astype(BF)
            value = value - piece.astype(F32)
            total = total + jnp.dot(piece, place[half], preferred_element_type=F32)
        return total

    for side, rows in ((0, ra), (1, rb)):
        first[side].wait()
        gather_y(side, jnp.dot(pick, rows[...].reshape(64, 1024), preferred_element_type=F32).astype(BF))
    bfull[pl.ds(pl.multiple_of(k * 512, 512), 512), :] = bo[:, pl.ds(pl.multiple_of(k * 512, 512), 512)]
    for c in range(3):
        for side in range(2):
            gather_xz(side, c)

    train = lax.broadcasted_iota(jnp.int32, (1, 512), 1)
    device = train // 4
    spot = train // 2 % 2 * 256 + device % 2 * 128 + device // 2 % 4 * 32 + device % 16 // 8 * 16
    spot = spot + device // 16 * 2 + train % 2
    row = lax.broadcasted_iota(jnp.int32, (512, 512), 0)
    place[...] = jnp.where(row == spot, 1.0, 0.0).astype(BF).reshape(2, 256, 512)
    local[5].wait()
    basis_copy.wait()
    swap(0)
    rotate(0)
    swap(1)
    swap(2)
    rotate(1)
    reduce_y(0)
    rotate(2)
    local[6].wait()
    for half, at in enumerate((k, other)):
        rows = eig[pl.ds(pl.multiple_of(at * 512, 512), 512), :]
        inverse[:, pl.ds(half * 512, 512)] = jnp.transpose(1.0 / (rows + damping), (1, 0))
    spread(0)
    reduce_y(1)
    reduce_y(2)
    spread_core(0)
    lay_query()
    spread(1)
    scale(0, 0, 8)
    spread(2)
    scale(0, 8, 16)
    scale(1, 0, 16)
    spread_core(1)
    lay_train(1)
    pair(1, 0, 8)
    spread_core(2)
    pair(1, 8, 16)
    share_near(0)
    lay_train(2)
    pair(2, 0, 16)
    share_near(1)
    share_plane(0)
    share_plane(1)
    total = in_order(summed(0), 0)
    total = total + in_order(summed(1), 1)
    out[...] = total * (1.0 / math.sqrt(D_IN * D_OUT * QBLOCK))


def shards(
    train_inputs,
    train_grads,
    query_inputs,
    query_grads,
    input_basis,
    output_basis,
    eigenvalues,
    query_starts,
    query_ends,
):
    vmem = pl.BlockSpec(memory_space=pltpu.VMEM)
    smem = pl.BlockSpec(memory_space=pltpu.SMEM)
    return pl.pallas_call(
        kernel,
        out_shape=jax.ShapeDtypeStruct((NQ, 512), F32),
        in_specs=[smem, smem] + [pl.BlockSpec(memory_space=pl.ANY)] * 7,
        out_specs=vmem,
        scratch_shapes=[
            pltpu.VMEM((4, 8192), BF),
            pltpu.VMEM((2, 8192), BF),
            pltpu.VMEM((4, 8192), BF),
            pltpu.VMEM((2, 8192), BF),
            pltpu.VMEM((1024, 512), BF),
            pltpu.VMEM((512, 1024), BF),
            pltpu.VMEM((1024, 512), F32),
            pltpu.VMEM((8, 8192), BF),
            pltpu.VMEM((8, 8192), BF),
            pltpu.VMEM((8, 8, 1024), BF),
            pltpu.VMEM((8, 8, 1024), BF),
            pltpu.VMEM((3, 2, 4, 2, 16, 1024), BF),
            pltpu.VMEM((3, 2, 4, 2, 16, 1024), BF),
            pltpu.VMEM((1024, 512), BF),
            pltpu.VMEM((3, 4, 256, 128), F32),
            pltpu.VMEM((3, 4, 256, 128), F32),
            pltpu.VMEM((3, 4, 256, 128), BF),
            pltpu.VMEM((3, 4, 256, 128), BF),
            pltpu.VMEM((3, 3, 256, 128), BF),
            pltpu.VMEM((3, 3, 256, 128), BF),
            pltpu.VMEM((256, 128), F32),
            pltpu.VMEM((256, 128), F32),
            pltpu.VMEM((2, 256, 128), BF),
            pltpu.VMEM((2, 256, 128), BF),
            pltpu.VMEM((2, 256, 128), BF),
            pltpu.VMEM((2, 256, 128), BF),
            pltpu.VMEM((3, 4, 256, 128), BF),
            pltpu.VMEM((3, 2, 4, 256, 128), BF),
            pltpu.VMEM((512, 1024), F32),
            pltpu.VMEM((512, 256), F32),
            pltpu.VMEM((256, 1024), BF),
            pltpu.VMEM((2, 512, 256), F32),
            pltpu.VMEM((2, 1024, 256), BF),
            pltpu.VMEM((NQ, 512, 1024), BF),
            pltpu.VMEM((2, NQ, 256), F32),
            pltpu.VMEM((128, 128), BF),
            pltpu.VMEM((2, 256, 512), BF),
            pltpu.VMEM((1, 256), jnp.int32),
            pltpu.VMEM((3, 8, NQ, 256), F32),
            pltpu.VMEM((3, 16, NQ, 256), F32),
            pltpu.SemaphoreType.DMA((7,)),
            pltpu.SemaphoreType.DMA((12,)),
            pltpu.SemaphoreType.DMA((51,)),
        ],
        compiler_params=pltpu.CompilerParams(
            collective_id=0, has_side_effects=True, vmem_limit_bytes=56 * 2**20
        ),
    )(
        query_starts, query_ends, train_inputs, query_inputs, train_grads, query_grads,
        input_basis, output_basis, eigenvalues,
    )


def solution(mesh):
    split = Mesh(mesh.devices.reshape(4, 2, 2, 4, 2), ALL)
    placed = (
        P(ROW + COL, None),
        P(ROW + COL, None),
        P(ROW + COL, None),
        P(ROW + COL, None),
        P(ROW, COL),
        P(COL, ROW),
        P(ROW, COL),
        P(),
        P(),
    )
    return jax.shard_map(shards, mesh=split, in_specs=placed, out_specs=P(), check_vma=False)
```

```python
import math

import jax
import jax.numpy as jnp
from jax import lax
from jax.experimental import pallas as pl
from jax.experimental.pallas import tpu as pltpu
from jax.sharding import Mesh
from jax.sharding import PartitionSpec as P

D_IN = 8192
D_OUT = 8192
QBLOCK = 128
NQ = 16
MESH = pl.DeviceIdType.MESH
ROW = ("x", "u")
COL = ("v", "z", "k")
ALL = ("x", "u", "v", "z", "k")
damping = 0.1
BF = jnp.bfloat16
F32 = jnp.float32


def send(src, dst, send_sem, recv_sem, device):
    copy = pltpu.make_async_remote_copy(
        src_ref=src,
        dst_ref=dst,
        send_sem=send_sem,
        recv_sem=recv_sem,
        device_id=device,
        device_id_type=MESH,
    )
    copy.start()
    return copy


def arrival(ref, send_sem, recv_sem, device):
    return pltpu.make_async_remote_copy(
        src_ref=ref,
        dst_ref=ref,
        send_sem=send_sem,
        recv_sem=recv_sem,
        device_id=device,
        device_id_type=MESH,
    )


def one_hot(rows, cols, source):
    row = lax.broadcasted_iota(jnp.int32, (rows, 1), 0)
    col = lax.broadcasted_iota(jnp.int32, (rows, cols), 1)
    return jnp.where(col == source(row), 1.0, 0.0).astype(BF)


def compact_source(row):
    chunk, inner = row // 16, row % 16
    first = jnp.where(chunk == 0, 4, 2 * chunk - 2)
    return inner // 2 * 8 + first + inner % 2


def swapped_source(row):
    outer, inner, j = row // 16, row // 2 % 8, row % 2
    return inner * 16 + outer * 2 + j


def device_of(row):
    k, z, v = row // 128, row // 32 % 4, row // 16 % 2
    x, u = row // 4 % 4, row // 2 % 2
    return 16 * (2 * x + u) + 8 * v + 2 * z + k


def tree(values):
    while len(values) > 1:
        values = [a + b for a, b in zip(values[::2], values[1::2])]
    return values[0]


def turned(block):
    return jnp.transpose(block.astype(F32), (1, 0))


def kernel(
    starts, ends, ti, qi, tg, qg, bi_hbm, bo_hbm, eig_hbm, out,
    tiv, qiv, tgv, qgv, bi, bo, eig,
    xi, gi, ra, rb, ai, ag, bfull, pi, pg, si, sg, ri, rg, yqi, yqg, yti, ytg, wti, wtg, hi, hg,
    inverse, a_query, g_query, a_train, g_train, scaled, acc, turn, place, true_rows, near_sums, plane_sums,
    lsem, ssem, rsem,
):
    x, u, v, z, k = (lax.axis_index(a) for a in ALL)
    r, p = x * 2 + u, v * 4 + z
    other = 1 - k
    near, plane = u * 4 + v * 2 + k, x * 4 + z

    def row_peer(d):
        q = lax.rem(r + d, 8)
        return q, {"x": q // 2, "u": lax.rem(q, 2)}

    def col_peer(d):
        q = lax.rem(p + d, 8)
        return q, {"v": q // 4, "z": lax.rem(q, 4)}

    def x_peer(d):
        return {"x": lax.rem(x + d, 4)}

    def z_peer(d):
        return {"z": lax.rem(z + d, 4)}

    def near_peer(d):
        q = lax.rem(near + d, 8)
        return {"u": q // 4, "v": lax.rem(q // 2, 2), "k": lax.rem(q, 2)}

    def plane_peer(d):
        q = lax.rem(plane + d, 16)
        return {"x": q // 4, "z": lax.rem(q, 4)}

    barrier = pltpu.get_barrier_semaphore()
    for d in range(1, 8):
        for peer in (row_peer(d)[1], col_peer(d)[1]):
            pl.semaphore_signal(barrier, inc=1, device_id=peer, device_id_type=MESH)
    pl.semaphore_signal(barrier, inc=1, device_id={"k": other}, device_id_type=MESH)

    local = []
    for i, (src, dst) in enumerate((
        (ti, tiv), (qi, qiv), (tg, tgv), (qg, qgv), (bo_hbm, bo), (bi_hbm, bi), (eig_hbm, eig)
    )):
        local.append(pltpu.make_async_copy(src, dst, lsem.at[i]))
        local[-1].start()
    for copy in local[:4]:
        copy.wait()
    for rows, train, query in ((xi, tiv, qiv), (gi, tgv, qgv)):
        rows[...] = jnp.concatenate(
            [train[...].astype(F32), query[...].astype(F32), jnp.zeros((2, D_IN), F32)], axis=0
        ).astype(BF)
    pl.semaphore_wait(barrier, 15)

    for d in range(1, 8):
        q, peer = row_peer(d)
        send(
            xi.at[:, pl.ds(pl.multiple_of(q * 1024, 1024), 1024)], ra.at[r],
            ssem.at[1], rsem.at[1], peer,
        )
        q, peer = col_peer(d)
        send(
            gi.at[:, pl.ds(pl.multiple_of(q * 1024, 1024), 1024)], rb.at[2 * z + v],
            ssem.at[2], rsem.at[2], peer,
        )
    first = (
        arrival(ra.at[0:7], ssem.at[1], rsem.at[1], row_peer(1)[1]),
        arrival(rb.at[0:7], ssem.at[2], rsem.at[2], col_peer(1)[1]),
    )
    ra[r] = xi[:, pl.ds(pl.multiple_of(r * 1024, 1024), 1024)]
    rb[2 * z + v] = gi[:, pl.ds(pl.multiple_of(p * 1024, 1024), 1024)]
    pick = one_hot(48, 64, compact_source)
    local[4].wait()
    basis_copy = send(
        bo.at[:, pl.ds(pl.multiple_of(other * 512, 512), 512)],
        bfull.at[pl.ds(pl.multiple_of(k * 512, 512), 512)],
        ssem.at[0], rsem.at[0], {"k": other},
    )
    turn[...] = one_hot(128, 128, swapped_source)
    lanes = lax.broadcasted_iota(jnp.int32, (1, 256), 1)
    true_rows[...] = 2 * device_of(lanes) + lanes % 2

    moving = {}

    def wait(*key):
        moving.pop(key).wait()

    def sems(side, c, step):
        return ssem.at[3 + side * 3 + c], rsem.at[3 + (side * 3 + c) * 7 + step]

    gathered = (ai, ag)
    gather_at = ((z, v), (x, u))
    gather_y_peer = ({"v": 1 - v}, {"u": 1 - u})
    gather_peer = (z_peer, x_peer)
    sum_at = (x, z)
    sum_name = ("x", "z")
    sum_y_peer = ({"u": 1 - u}, {"v": 1 - v})
    part = (pi, pg)
    small = (si, sg)
    got = (ri, rg)
    wide_y = (yqi, yqg)
    mine_y = (wti, wtg)
    their_y = (yti, ytg)

    def gather_y(side, rows):
        at = gather_at[side]
        for c in range(3):
            ref = gathered[side].at[c, k, at[0], at[1]]
            ref[...] = rows[16 * c : 16 * c + 16]
            moving[side, c, 0] = send(ref, ref, *sems(side, c, 0), gather_y_peer[side])

    def gather_xz(side, c):
        wait(side, c, 0)
        ref = gathered[side].at[c, k, gather_at[side][0]]
        for d in (2, 1, 3):
            send(ref, ref, *sems(side, c, 1), gather_peer[side](d))
        moving[side, c, 1] = arrival(
            gathered[side].at[c, k, 0:3], *sems(side, c, 1), gather_peer[side](1)
        )

    def swap(c):
        for side in range(2):
            wait(side, c, 1)
            ref = gathered[side].at[c, k]
            moving[side, c, 2] = send(ref, ref, *sems(side, c, 2), {"k": other})

    def rotate(c):
        for side in range(2):
            wait(side, c, 2)
            if side == 0:
                blocks = [(0, 256, ai[c].reshape(256, 1024), bi)]
            else:
                blocks = [
                    (h * 128, 128, jnp.dot(
                        turn[...], ag[c, h].reshape(128, 1024), preferred_element_type=F32
                    ).astype(BF), bfull)
                    for h in range(2)
                ]
            for low, size, rows, basis in blocks:
                value = jnp.dot(rows, basis[...], preferred_element_type=F32)
                for b in range(4):
                    piece = value[:, b * 128 : (b + 1) * 128]
                    part[side][c, b, pl.ds(low, size)] = piece
                    small[side][c, b, pl.ds(low, size)] = piece.astype(BF)
            for d in (2, 1, 3):
                q = lax.rem(sum_at[side] + d, 4)
                send(
                    small[side].at[c, q], got[side].at[c, d - 1], *sems(side, c, 3),
                    {sum_name[side]: q},
                )
            moving[side, c, 3] = arrival(got[side].at[c], *sems(side, c, 3), {sum_name[side]: q})

    def reduce_y(c):
        for side in range(2):
            wait(side, c, 3)
            at = sum_at[side]
            value = part[side][c, at]
            for d in range(3):
                value = value + got[side][c, d].astype(F32)
            part[side][c, at] = value
            if c == 0:
                src, dst = part[side].at[c, at], wide_y[side]
            else:
                mine_y[side][c - 1] = value.astype(BF)
                src, dst = mine_y[side].at[c - 1], their_y[side].at[c - 1]
            moving[side, c, 4] = send(src, dst, *sems(side, c, 4), sum_y_peer[side])

    def spread(c):
        for side in range(2):
            wait(side, c, 4)
            at = sum_at[side]
            more = wide_y[side][...] if c == 0 else their_y[side][c - 1].astype(F32)
            ref = hi.at[c, at] if side == 0 else hg.at[c, k, at]
            ref[...] = (part[side][c, at] + more).astype(BF)
            peer = x_peer if side == 0 else z_peer
            for d in (2, 1, 3):
                send(ref, ref, *sems(side, c, 5), peer(d))
            three = hi.at[c, 0:3] if side == 0 else hg.at[c, k, 0:3]
            moving[side, c, 5] = arrival(three, *sems(side, c, 5), peer(1))

    def spread_core(c):
        wait(1, c, 5)
        moving[1, c, 6] = send(hg.at[c, k], hg.at[c, k], *sems(1, c, 6), {"k": other})

    def lay_query():
        wait(0, 0, 5)
        for b in range(4):
            a_query[pl.ds(b * 128, 128), :] = turned(hi[0, b])

    def scale(half, low, high):
        if low == 0:
            if half == 1:
                wait(1, 0, 6)
            for b in range(4):
                g_query[:, pl.ds(half * 512 + b * 128, 128)] = hg[0, (k, other)[half], b]

        def body(q, carry):
            inside = (true_rows[...] >= starts[q]) & (true_rows[...] < ends[q])
            rows = jnp.where(inside, a_query[...], 0.0).astype(BF)
            for o in range(2):
                at = pl.ds(half * 512 + o * 256, 256)
                outer = jnp.dot(rows, g_query[:, at], preferred_element_type=F32)
                scaled[q, :, at] = (outer * inverse[:, at]).astype(BF)
            return carry

        lax.fori_loop(low, high, body, 0, unroll=high - low)

    def lay_train(c):
        wait(0, c, 5)
        for b in range(4):
            a_train[c - 1, pl.ds(b * 128, 128), :] = turned(hi[c, b])
        wait(1, c, 6)
        for b in range(4):
            for s in range(2):
                block = hg[c, (k, other)[s], b]
                g_train[c - 1, pl.ds(s * 512 + b * 128, 128), :] = turned(block).astype(BF)

    def pair(c, low, high):
        def body(q, carry):
            paired = jnp.dot(scaled[q], g_train[c - 1], preferred_element_type=F32)
            acc[c - 1, pl.ds(q, 1), :] = jnp.sum(paired * a_train[c - 1], axis=0, keepdims=True)
            return carry

        lax.fori_loop(low, high, body, 0, unroll=high - low)

    pieces = ((0, 0, 16), (1, 0, 16))

    def share_near(i):
        half, low, size = pieces[i]
        rows = pl.ds(0, size)
        near_sums[i, near, rows, :] = acc[half, pl.ds(low, size), :]
        ref = near_sums.at[i, near, rows]
        pair_of = (ssem.at[9 + i], rsem.at[45 + i])
        for d in range(1, 8):
            send(ref, ref, *pair_of, near_peer(d))
        moving["near", i] = arrival(near_sums.at[i, 0:7, rows], *pair_of, near_peer(1))

    def share_plane(i):
        wait("near", i)
        rows = pl.ds(0, pieces[i][2])
        plane_sums[i, plane, rows, :] = tree([near_sums[i, j, rows, :] for j in range(8)])
        ref = plane_sums.at[i, plane, rows]
        pair_of = (ssem.at[9 + i], rsem.at[48 + i])
        for d in range(1, 16):
            send(ref, ref, *pair_of, plane_peer(d))
        moving["plane", i] = arrival(plane_sums.at[i, 0:15, rows], *pair_of, plane_peer(1))

    def summed(i):
        wait("plane", i)
        rows = pl.ds(0, pieces[i][2])
        return tree([plane_sums[i, j, rows, :] for j in range(16)])

    def in_order(value, half):
        total = 0.0
        for _ in range(3):
            piece = value.astype(BF)
            value = value - piece.astype(F32)
            total = total + jnp.dot(piece, place[half], preferred_element_type=F32)
        return total

    for side, rows in ((0, ra), (1, rb)):
        first[side].wait()
        gather_y(side, jnp.dot(pick, rows[...].reshape(64, 1024), preferred_element_type=F32).astype(BF))
    bfull[pl.ds(pl.multiple_of(k * 512, 512), 512), :] = bo[:, pl.ds(pl.multiple_of(k * 512, 512), 512)]
    for c in range(3):
        for side in range(2):
            gather_xz(side, c)

    train = lax.broadcasted_iota(jnp.int32, (1, 512), 1)
    device = train // 4
    spot = train // 2 % 2 * 256 + device % 2 * 128 + device // 2 % 4 * 32 + device % 16 // 8 * 16
    spot = spot + device // 16 * 2 + train % 2
    row = lax.broadcasted_iota(jnp.int32, (512, 512), 0)
    place[...] = jnp.where(row == spot, 1.0, 0.0).astype(BF).reshape(2, 256, 512)
    local[5].wait()
    basis_copy.wait()
    swap(0)
    rotate(0)
    swap(1)
    swap(2)
    rotate(1)
    reduce_y(0)
    rotate(2)
    local[6].wait()
    for half, at in enumerate((k, other)):
        rows = eig[pl.ds(pl.multiple_of(at * 512, 512), 512), :]
        inverse[:, pl.ds(half * 512, 512)] = jnp.transpose(1.0 / (rows + damping), (1, 0))
    spread(0)
    reduce_y(1)
    reduce_y(2)
    spread_core(0)
    lay_query()
    spread(1)
    scale(0, 0, 8)
    spread(2)
    scale(0, 8, 16)
    scale(1, 0, 8)
    spread_core(1)
    scale(1, 8, 16)
    lay_train(1)
    pair(1, 0, 8)
    spread_core(2)
    pair(1, 8, 16)
    share_near(0)
    lay_train(2)
    pair(2, 0, 16)
    share_near(1)
    share_plane(0)
    share_plane(1)
    total = in_order(summed(0), 0)
    total = total + in_order(summed(1), 1)
    out[...] = total * (1.0 / math.sqrt(D_IN * D_OUT * QBLOCK))


def shards(
    train_inputs,
    train_grads,
    query_inputs,
    query_grads,
    input_basis,
    output_basis,
    eigenvalues,
    query_starts,
    query_ends,
):
    vmem = pl.BlockSpec(memory_space=pltpu.VMEM)
    smem = pl.BlockSpec(memory_space=pltpu.SMEM)
    return pl.pallas_call(
        kernel,
        out_shape=jax.ShapeDtypeStruct((NQ, 512), F32),
        in_specs=[smem, smem] + [pl.BlockSpec(memory_space=pl.ANY)] * 7,
        out_specs=vmem,
        scratch_shapes=[
            pltpu.VMEM((4, 8192), BF),
            pltpu.VMEM((2, 8192), BF),
            pltpu.VMEM((4, 8192), BF),
            pltpu.VMEM((2, 8192), BF),
            pltpu.VMEM((1024, 512), BF),
            pltpu.VMEM((512, 1024), BF),
            pltpu.VMEM((1024, 512), F32),
            pltpu.VMEM((8, 8192), BF),
            pltpu.VMEM((8, 8192), BF),
            pltpu.VMEM((8, 8, 1024), BF),
            pltpu.VMEM((8, 8, 1024), BF),
            pltpu.VMEM((3, 2, 4, 2, 16, 1024), BF),
            pltpu.VMEM((3, 2, 4, 2, 16, 1024), BF),
            pltpu.VMEM((1024, 512), BF),
            pltpu.VMEM((3, 4, 256, 128), F32),
            pltpu.VMEM((3, 4, 256, 128), F32),
            pltpu.VMEM((3, 4, 256, 128), BF),
            pltpu.VMEM((3, 4, 256, 128), BF),
            pltpu.VMEM((3, 3, 256, 128), BF),
            pltpu.VMEM((3, 3, 256, 128), BF),
            pltpu.VMEM((256, 128), F32),
            pltpu.VMEM((256, 128), F32),
            pltpu.VMEM((2, 256, 128), BF),
            pltpu.VMEM((2, 256, 128), BF),
            pltpu.VMEM((2, 256, 128), BF),
            pltpu.VMEM((2, 256, 128), BF),
            pltpu.VMEM((3, 4, 256, 128), BF),
            pltpu.VMEM((3, 2, 4, 256, 128), BF),
            pltpu.VMEM((512, 1024), F32),
            pltpu.VMEM((512, 256), F32),
            pltpu.VMEM((256, 1024), BF),
            pltpu.VMEM((2, 512, 256), F32),
            pltpu.VMEM((2, 1024, 256), BF),
            pltpu.VMEM((NQ, 512, 1024), BF),
            pltpu.VMEM((2, NQ, 256), F32),
            pltpu.VMEM((128, 128), BF),
            pltpu.VMEM((2, 256, 512), BF),
            pltpu.VMEM((1, 256), jnp.int32),
            pltpu.VMEM((3, 8, NQ, 256), F32),
            pltpu.VMEM((3, 16, NQ, 256), F32),
            pltpu.SemaphoreType.DMA((7,)),
            pltpu.SemaphoreType.DMA((12,)),
            pltpu.SemaphoreType.DMA((51,)),
        ],
        compiler_params=pltpu.CompilerParams(
            collective_id=0, has_side_effects=True, vmem_limit_bytes=56 * 2**20
        ),
    )(
        query_starts, query_ends, train_inputs, query_inputs, train_grads, query_grads,
        input_basis, output_basis, eigenvalues,
    )


def solution(mesh):
    split = Mesh(mesh.devices.reshape(4, 2, 2, 4, 2), ALL)
    placed = (
        P(ROW + COL, None),
        P(ROW + COL, None),
        P(ROW + COL, None),
        P(ROW + COL, None),
        P(ROW, COL),
        P(COL, ROW),
        P(ROW, COL),
        P(),
        P(),
    )
    return jax.shard_map(shards, mesh=split, in_specs=placed, out_specs=P(), check_vma=False)
```
